512 devices in a mesh: xy: 128 (over x, y_hi, z, core), gz: 4 (over y_lo).
Axes of the slice: x: 4, y: 8 (y_hi: 2, y_lo: 4; y = y_hi * 4 + y_lo), z: 8, core: 2. Of those that a mesh axis runs over, the one named last changes fastest.
Arguments:
- density: float32 [16384, 2048], P('xy', 'gz'), may hold values from 0 to 1
- cotangent: float32 [6, 16, 2048, 256], P(None, 'gz', 'xy'), may hold values from -6 to 6
- slope: int32 [16], P('gz'), may hold values from 0 to 4
- layer_block: int32 [16], P('gz'), may hold values from 0 to 3
- block_eps: float32 [4, 2], replicated, may hold values from 1.5 to 12
Outputs:
- grad_filtered: float32 [16384, 2048], P('xy', 'gz')
- grad_density: float32 [16384, 2048], P('xy', 'gz')
The draws below stay inside these ranges and needn't reach their ends.
All inputs are finite; a program needn't handle non-finite values.
Results may differ from the reference program's by a relative error of at most 0.0003.
Values sent between devices are 32-bit elements; how exact they have to be, the bound alone decides.
No kernel may reach another device: no remote copies, remote signals or barrier semaphores. Data moves between devices by JAX's collectives and lax.ppermute only.
A program may use at most 64 MiB of HBM per device.

```python
import math
import jax
import jax.numpy as jnp
from jax import lax

SUB = 8
RADIUS = 32
MATS = 4
SLOPES = 5
NX = 2048
NY = 256
LAYERS = 16
NXD = 16384
NYD = 2048


def touch_ends(drawn, stream_key, low, largest):
    place = [jax.random.randint(jax.random.fold_in(stream_key, axis), (), 0, length) for axis, length in enumerate(drawn.shape)]
    main_axis = drawn.shape.index(max(drawn.shape))
    neighbour = place[:main_axis] + [(place[main_axis] + 1) % drawn.shape[main_axis]] + place[main_axis + 1:]
    return drawn.at[tuple(place)].set(low).at[tuple(neighbour)].set(largest)


def block_scale(rng, extent, shards, least, largest):
    def one(axis_at, shards_of):
        draws = jax.random.uniform(jax.random.fold_in(jax.random.fold_in(rng, 6), axis_at), (shards_of,), jnp.float32, least / len(shards), largest / len(shards))
        return jnp.repeat(jnp.exp(draws), extent[axis_at] // shards_of).reshape((-1,) + (1,) * (len(extent) - axis_at - 1))

    factor_of = one(*shards[0])
    for cut in shards[1:]:
        factor_of = factor_of * one(*cut)
    return factor_of


def scatter_about(stream_key, shape, spread, most, pieces=(), kind=jnp.bfloat16):
    factor_of = block_scale(stream_key, shape, pieces, -0.22, 0.18) if pieces else 1.0
    array = jax.random.normal(stream_key, shape, jnp.float32) * spread * factor_of
    return jnp.minimum(jnp.maximum(array, -most), most).astype(kind)


def setup_inputs(seed: int = 0) -> dict:
    seeds = jax.random.split(jax.random.key(seed), 6)
    return {
        "density": jnp.clip(1.0 * jax.random.uniform(seeds[0], (NXD, NYD), jnp.float32) ** block_scale(seeds[0], (NXD, NYD), ((0, 128), (1, 4)), -0.2, 0.2), 0.0, 1.0),
        "cotangent": scatter_about(seeds[1], (6, LAYERS, NX, NY), 1.0, 6.0, ((1, 4), (2, 128)), jnp.float32),
        "slope": touch_ends(jax.random.randint(seeds[2], (LAYERS,), 0, SLOPES), jax.random.fold_in(seeds[2], 1), 0, SLOPES - 1).astype(jnp.int32),
        "layer_block": touch_ends(jax.random.randint(seeds[3], (LAYERS,), 0, MATS), jax.random.fold_in(seeds[3], 1), 0, MATS - 1).astype(jnp.int32),
        "block_eps": jnp.clip(jnp.exp(jax.random.uniform(seeds[4], (MATS, 2), jnp.float32, math.log(1.5), math.log(12.0))), 1.5, 12.0),
    }


def smooth(field):
    taps = jnp.arange(2 * RADIUS + 1)
    weights = (RADIUS + 1 - jnp.abs(taps - RADIUS)).astype(jnp.float32) / float((RADIUS + 1) ** 2)
    padded = jnp.pad(field, ((0, 0), (RADIUS, RADIUS)))
    width = field.shape[1]
    across = jnp.zeros_like(field)
    for k in range(2 * RADIUS + 1):
        across = across + weights[k] * padded[:, k:k + width]
    padded = jnp.pad(across, ((RADIUS, RADIUS), (0, 0)))
    height = field.shape[0]
    result = jnp.zeros_like(field)
    for k in range(2 * RADIUS + 1):
        result = result + weights[k] * padded[k:k + height, :]
    return result

def cell_tensor(filtered, params):
    eta, lift, eps_one, eps_two = (params[0], params[1], params[2], params[3])
    fill = jax.nn.sigmoid(32.0 * (filtered - eta))
    blocks = fill.reshape(NX, SUB, NY, SUB)
    offsets = (2.0 * jnp.arange(SUB).astype(jnp.float32) + 1.0 - SUB) / 2.0
    frac = lax.optimization_barrier(jnp.mean(blocks, axis=(1, 3)))
    grad_x = lax.optimization_barrier(jnp.mean(blocks * offsets[None, :, None, None], axis=(1, 3)))
    grad_y = lax.optimization_barrier(jnp.mean(blocks * offsets[None, None, None, :], axis=(1, 3)))
    normsq = grad_x * grad_x + grad_y * grad_y + lift * lift
    mean_eps = eps_two + frac * (eps_one - eps_two)
    mean_inv = 1.0 / eps_two + frac * (1.0 / eps_one - 1.0 / eps_two)
    weight = (1.0 / mean_inv - mean_eps) / normsq
    lifted = lift * jnp.ones_like(grad_x)
    return jnp.stack([mean_eps + weight * grad_x * grad_x, mean_eps + weight * grad_y * grad_y, mean_eps + weight * lifted * lifted, weight * grad_x * grad_y, weight * grad_x * lifted, weight * grad_y * lifted])

def reference(density, cotangent, slope, layer_block, block_eps):
    filtered = smooth(density)
    level = slope.astype(jnp.float32)
    onehot = (layer_block[:, None] == jnp.arange(MATS)[None, :]).astype(jnp.float32)
    pairs = jnp.dot(onehot, block_eps, precision=lax.Precision.HIGHEST)
    table = jnp.stack([0.5 + 0.02 * (level - 2.0), 0.2 * (1.0 + level), pairs[:, 0], pairs[:, 1]])

    def step(total, index):
        params = table[:, index]
        pullback = jax.vjp(lambda field: cell_tensor(field, params), filtered)[1]
        return (total + pullback(cotangent[:, index])[0], None)
    grad_filtered, unused = lax.scan(step, jnp.zeros_like(filtered), jnp.arange(LAYERS))
    return (grad_filtered, smooth(grad_filtered))
```

```python
import functools
import math

import jax
import jax.numpy as jnp
from jax import lax
from jax.experimental import pallas as pl
from jax.experimental.pallas import tpu as pltpu
from jax.sharding import PartitionSpec as P

SUB = 8
RADIUS = 32
MATS = 4
SLOPES = 5
SCALE = 1.0 / float((RADIUS + 1) ** 2)
BF = jnp.bfloat16
F32 = jnp.float32
VMEM = pl.BlockSpec(memory_space=pltpu.VMEM)
SMEM = pl.BlockSpec(memory_space=pltpu.SMEM)
LIMIT = 24 << 20

HEIGHT = 128
WIDTH = 512
WIDE = WIDTH + 2 * RADIUS
CELLS = WIDE // SUB
ROWS = 224


def iota(shape, dim):
    return lax.broadcasted_iota(jnp.int32, shape, dim)


def parts_of(value, count):
    parts = []
    for index in range(count):
        part = value.astype(BF)
        parts.append(part)
        if index + 1 < count:
            value = value - part.astype(F32)
    return parts


def band(rows, cols):
    offset = iota((rows, cols), 1) - iota((rows, cols), 0) - RADIUS
    return jnp.maximum(RADIUS + 1 - jnp.abs(offset), 0).astype(F32).astype(BF)


def dot(a, b):
    return jnp.dot(a, b, preferred_element_type=F32)


def place_lanes():
    return (iota((1, HEIGHT), 1) % SUB).astype(F32) - 3.5


def call(body, name, outs, scratch, flops, moved, *args, smem=()):
    return pl.pallas_call(
        body,
        name=name,
        out_shape=[jax.ShapeDtypeStruct(shape, F32) for shape in outs],
        in_specs=[SMEM if index in smem else VMEM for index in range(len(args))],
        out_specs=[VMEM for _ in outs],
        scratch_shapes=[pltpu.VMEM(shape, F32) for shape in scratch],
        compiler_params=pltpu.CompilerParams(vmem_limit_bytes=LIMIT),
        cost_estimate=pl.CostEstimate(flops=flops, bytes_accessed=moved, transcendentals=0),
    )(*args)


def pack_body(slope, block, eps, cot, send):
    low = iota((SUB, HEIGHT), 0) < 4
    zero = jnp.zeros((SUB, HEIGHT), F32)
    for slab in range(3):
        turned = cot[slab * 128 : slab * 128 + 128, :].T
        for owner in range(4):
            first, base = (64 * owner, 72 * slab)
            send[owner, base : base + 64, :] = turned[first : first + 64]
            after = zero if owner == 3 else turned[first + 64 : first + 72]
            before = zero if owner == 0 else turned[first - 8 : first]
            send[owner, base + 64 : base + 72, :] = jnp.where(low, after, before)
    layer = (iota((SUB, HEIGHT), 1) % 64) // 16
    row = iota((SUB, HEIGHT), 0)
    table = zero
    for index in range(4):
        one = eps[block[index], 0]
        two = eps[block[index], 1]
        level = slope[index].astype(F32)
        column = jnp.where(row == 0, level, jnp.where(row == 1, one, jnp.where(row == 2, two, 0.0)))
        table = jnp.where(layer == index, column, table)
    for owner in range(4):
        send[owner, 216:224, :] = table


def rows_body(top, own, bottom, out, first, last):
    padded = jnp.concatenate([top[...], own[...], bottom[...]], axis=0)
    matrix = band(HEIGHT, HEIGHT + 2 * RADIUS)
    total = None
    for part in parts_of(padded, 3):
        term = dot(matrix, part)
        total = term if total is None else total + term
    turned = (total * SCALE).T
    out[...] = turned
    first[...] = turned[:64]
    last[...] = turned[WIDTH - 64 :]


def forward_body(left, own, right, expo, pooled, natural):
    padded = jnp.concatenate([left[...], own[...], right[...]], axis=0)
    padded = jnp.concatenate(parts_of(padded, 3), axis=1)
    matrix = band(192, 256)
    for block in range(3):
        wide = dot(matrix, padded[192 * block : 192 * block + 256])
        field = (wide[:, :128] + wide[:, 128:256] + wide[:, 256:]) * SCALE
        value = jnp.exp(16.0 - 32.0 * field)
        if block == 0:
            natural[WIDTH + RADIUS : WIDE, :] = value[:RADIUS]
            natural[: 192 - RADIUS, :] = value[RADIUS:]
        else:
            natural[192 * block - RADIUS : 192 * block - RADIUS + 192, :] = value
    for q in range(SUB):
        expo[q] = natural[pl.ds(q, CELLS, stride=SUB), :]
    place = place_lanes()
    stacks = []
    for s in range(SLOPES):
        factor = math.exp(0.64 * (s - 2))
        mean = jnp.zeros((CELLS, HEIGHT), F32)
        slant = jnp.zeros((CELLS, HEIGHT), F32)
        for q in range(SUB):
            fill = 1.0 / (1.0 + factor * expo[q])
            mean = mean + fill
            slant = slant + (q - 3.5) * fill
        stacks += [mean, mean * place, slant]
    stacks.append(jnp.zeros((SUB, HEIGHT), F32))
    rows = jnp.concatenate(parts_of(jnp.concatenate(stacks, axis=0), 2), axis=1)
    base = ((iota((256, 256), 0) % 128) // SUB == iota((256, 256), 1) % 16).astype(F32).astype(BF)
    pooled[...] = dot(rows, base) * (1.0 / 64.0)


def backward_body(expo, pooled, got, out, turned, top, bottom, natural):
    half = iota((1, 128), 1) < 64
    def pair(a, b):
        return jnp.where(half, a, b)

    def line(row):
        value = [got[g, row : row + 1, :] for g in range(4)]
        return jnp.concatenate([pair(value[0], value[1]), pair(value[2], value[3])], axis=1)

    level, eps_one, eps_two = (line(216), line(217), line(218))
    comps = []
    for slab in range(3):
        value = [got[g, 72 * slab : 72 * slab + 72, :] for g in range(4)]
        swapped = [pltpu.roll(v, 64, 1) for v in value]
        comps.append(jnp.concatenate([pair(value[0], swapped[1]), pair(value[2], swapped[3])], axis=1))
        comps.append(jnp.concatenate([pair(swapped[0], value[1]), pair(swapped[2], value[3])], axis=1))
    cxx, cyy, czz, cxy, cxz, cyz = comps
    frac = jnp.zeros((CELLS, 256), F32)
    grad_x = jnp.zeros((CELLS, 256), F32)
    grad_y = jnp.zeros((CELLS, 256), F32)
    masks = []
    for s in range(SLOPES):
        mask = level == float(s)
        masks.append(mask)
        frac = jnp.where(mask, pooled[216 * s : 216 * s + 72, :], frac)
        grad_x = jnp.where(mask, pooled[216 * s + 72 : 216 * s + 144, :], grad_x)
        grad_y = jnp.where(mask, pooled[216 * s + 144 : 216 * s + 216, :], grad_y)
    lift = 0.2 * (1.0 + level)
    slope_mean = eps_one - eps_two
    inv_two = 1.0 / eps_two
    slope_inv = 1.0 / eps_one - inv_two
    mean_eps = eps_two + frac * slope_mean
    harmonic = 1.0 / (inv_two + frac * slope_inv)
    inv_norm = 1.0 / (grad_x * grad_x + grad_y * grad_y + lift * lift)
    weight = (harmonic - mean_eps) * inv_norm
    along_x = cxx * grad_x + cxy * grad_y + cxz * lift
    along_y = cyy * grad_y + cyz * lift
    quad = grad_x * along_x + grad_y * along_y + czz * (lift * lift)
    trace = cxx + cyy + czz
    d_frac = trace * slope_mean - quad * inv_norm * (harmonic * harmonic * slope_inv + slope_mean)
    shared = 2.0 * inv_norm * quad
    d_x = weight * (along_x + cxx * grad_x - grad_x * shared)
    d_y = weight * (along_y + cyy * grad_y + cxy * grad_x - grad_y * shared)
    stack = jnp.concatenate([d_frac, d_x, d_y, jnp.zeros((SUB, 256), F32)], axis=0) * 0.5
    high, low = parts_of(stack, 2)
    spread = (iota((256, HEIGHT), 0) % 16 == iota((256, HEIGHT), 1) // SUB).astype(F32).astype(BF)
    place = place_lanes()
    flat, tilt = ([], [])
    for mask in masks:
        keep = jnp.where(mask, 1.0, 0.0).astype(BF)
        both = dot(high * keep, spread) + dot(low * keep, spread)
        flat.append(both[:72] + place * both[72:144])
        tilt.append(both[144:216])
    for q in range(SUB):
        total = jnp.zeros((CELLS, HEIGHT), F32)
        for s in range(SLOPES):
            scaled = math.exp(0.64 * (s - 2)) * expo[q]
            fill = 1.0 / (1.0 + scaled)
            total = total + (fill * fill * scaled) * (flat[s] + (q - 3.5) * tilt[s])
        natural[pl.ds(q, CELLS, stride=SUB), :] = total
    out[...] = natural[:WIDTH, :].T
    matrix = band(192, 256)
    pieces = []
    for block in range(3):
        count = 192 if block < 2 else 128
        if block == 0:
            window = jnp.concatenate([natural[WIDTH + RADIUS : WIDE, :], natural[:224, :]], axis=0)
        else:
            window = natural[192 * block - RADIUS : 192 * block + count + RADIUS, :]
        wide = dot(matrix[:count, : count + 64], jnp.concatenate(parts_of(window, 2), axis=1))
        pieces.append((wide[:, :128] + wide[:, 128:]) * SCALE)
    result = jnp.concatenate(pieces, axis=0).T
    turned[...] = result
    top[...] = result[:RADIUS]
    bottom[...] = result[HEIGHT - RADIUS :]


def last_body(top, own, bottom, out):
    padded = jnp.concatenate([top[...], own[...], bottom[...]], axis=0)
    matrix = band(HEIGHT, HEIGHT + 2 * RADIUS)
    high, low = parts_of(padded, 2)
    out[...] = (dot(matrix, high) + dot(matrix, low)) * SCALE


def exchange(leading, trailing, axis):
    count = lax.axis_size(axis)
    up = [(i, i + 1) for i in range(count - 1)]
    down = [(j, i) for i, j in up]
    return (lax.ppermute(trailing, axis, up), lax.ppermute(leading, axis, down))


def on_device(density, cotangent, slope, layer_block, block_eps):
    flat = cotangent.reshape(384, 256)
    (send,) = call(pack_body, "pack", [(4, ROWS, 128)], [], 10**6, 10**6, slope, layer_block, block_eps, flat, smem=(0, 1, 2))
    got = lax.all_to_all(send, "gz", 0, 0, tiled=True)
    before, after = exchange(density[:RADIUS], density[HEIGHT - RADIUS :], "xy")
    across, first, last = call(rows_body, "rows", [(WIDTH, HEIGHT), (64, HEIGHT), (64, HEIGHT)], [], 10**8, 10**6, before, density, after)
    left, right = exchange(first, last, "gz")
    expo, pooled = call(forward_body, "forward", [(SUB, CELLS, HEIGHT), (1088, 256)], [(WIDE, HEIGHT)], 10**8, 2 * 10**6, left, across, right)
    own, turned, top, bottom = call(
        backward_body, "backward", [(HEIGHT, WIDTH), (HEIGHT, WIDTH), (RADIUS, WIDTH), (RADIUS, WIDTH)], [(WIDE, HEIGHT)], 10**8, 3 * 10**6, expo, pooled, got
    )
    before, after = exchange(top, bottom, "xy")
    (result,) = call(last_body, "last", [(HEIGHT, WIDTH)], [], 10**8, 10**6, before, turned, after)
    return (own, result)


def solution(mesh):
    return jax.shard_map(
        on_device,
        mesh=mesh,
        in_specs=(P("xy", "gz"), P(None, "gz", "xy", None), P("gz"), P("gz"), P()),
        out_specs=(P("xy", "gz"), P("xy", "gz")),
        check_vma=False,
    )
```

```python
import math

import jax
import jax.numpy as jnp
from jax import lax
from jax.experimental import pallas as pl
from jax.experimental.pallas import tpu as pltpu
from jax.sharding import PartitionSpec as P

SUB = 8
RADIUS = 32
SLOPES = 5
SCALE = 1.0 / float((RADIUS + 1) ** 2)
BF = jnp.bfloat16
F32 = jnp.float32
VMEM = pl.BlockSpec(memory_space=pltpu.VMEM)
SMEM = pl.BlockSpec(memory_space=pltpu.SMEM)
LIMIT = 24 << 20

HEIGHT = 128
WIDTH = 512
WIDE = WIDTH + 2 * RADIUS
CELLS = WIDE // SUB
ROWS = 224


def iota(shape, dim):
    return lax.broadcasted_iota(jnp.int32, shape, dim)


def parts_of(value, count):
    parts = []
    for index in range(count):
        part = value.astype(BF)
        parts.append(part)
        if index + 1 < count:
            value = value - part.astype(F32)
    return parts


def band(rows, cols):
    offset = iota((rows, cols), 1) - iota((rows, cols), 0) - RADIUS
    return jnp.maximum(RADIUS + 1 - jnp.abs(offset), 0).astype(F32).astype(BF)


def dot(a, b):
    return jnp.dot(a, b, preferred_element_type=F32)


def place_lanes():
    return (iota((1, HEIGHT), 1) % SUB).astype(F32) - 3.5


def call(body, outs, scratch, flops, moved, *args, smem=()):
    return pl.pallas_call(
        body,
        out_shape=[jax.ShapeDtypeStruct(shape, F32) for shape in outs],
        in_specs=[SMEM if index in smem else VMEM for index in range(len(args))],
        out_specs=[VMEM for _ in outs],
        scratch_shapes=[pltpu.VMEM(shape, F32) for shape in scratch],
        compiler_params=pltpu.CompilerParams(vmem_limit_bytes=LIMIT),
        cost_estimate=pl.CostEstimate(flops=flops, bytes_accessed=moved, transcendentals=0),
    )(*args)


def pack_body(slope_hbm, block_hbm, eps_hbm, cot_hbm, send, slope, block, eps, cot, sems):
    small = [
        pltpu.make_async_copy(source, target, sems.at[3 + index])
        for index, (source, target) in enumerate([(slope_hbm, slope), (block_hbm, block), (eps_hbm, eps)])
    ]
    slabs = [
        pltpu.make_async_copy(cot_hbm.at[pl.ds(128 * slab, 128)], cot.at[pl.ds(128 * slab, 128)], sems.at[slab])
        for slab in range(3)
    ]
    for copy in slabs + small:
        copy.start()
    low = iota((SUB, HEIGHT), 0) < 4
    zero = jnp.zeros((SUB, HEIGHT), F32)
    for slab in range(3):
        slabs[slab].wait()
        turned = cot[slab * 128 : slab * 128 + 128, :].T
        for owner in range(4):
            first, base = (64 * owner, 72 * slab)
            send[owner, base : base + 64, :] = turned[first : first + 64]
            after = zero if owner == 3 else turned[first + 64 : first + 72]
            before = zero if owner == 0 else turned[first - 8 : first]
            send[owner, base + 64 : base + 72, :] = jnp.where(low, after, before)
    for copy in small:
        copy.wait()
    layer = (iota((SUB, HEIGHT), 1) % 64) // 16
    row = iota((SUB, HEIGHT), 0)
    table = zero
    for index in range(4):
        one = eps[0, block[index]]
        two = eps[1, block[index]]
        level = slope[index].astype(F32)
        column = jnp.where(row == 0, level, jnp.where(row == 1, one, jnp.where(row == 2, two, 0.0)))
        table = jnp.where(layer == index, column, table)
    for owner in range(4):
        send[owner, 216:224, :] = table


def odd(axis):
    return lax.rem(lax.axis_index(axis), 2) == 1


def sides(axis, near, far):
    return (jnp.where(odd(axis), near, far), jnp.where(odd(axis), far, near))


def rows_body(near, own, far, out, to_near, to_far):
    before, after = sides("xy", near[...], far[...])
    padded = jnp.concatenate([before, own[...], after], axis=0)
    matrix = band(HEIGHT, HEIGHT + 2 * RADIUS)
    total = None
    for part in parts_of(padded, 3):
        term = dot(matrix, part)
        total = term if total is None else total + term
    turned = (total * SCALE).T
    out[...] = turned
    to_near[...], to_far[...] = sides("gz", turned[:64], turned[WIDTH - 64 :])


def forward_body(near, own, far, expo, pooled, natural):
    left, right = sides("gz", near[...], far[...])
    padded = jnp.concatenate([left, own[...], right], axis=0)
    padded = jnp.concatenate(parts_of(padded, 3), axis=1)
    matrix = band(192, 256)
    for block in range(3):
        wide = dot(matrix, padded[192 * block : 192 * block + 256])
        field = (wide[:, :128] + wide[:, 128:256] + wide[:, 256:]) * SCALE
        value = jnp.exp(16.0 - 32.0 * field)
        if block == 0:
            natural[WIDTH + RADIUS : WIDE, :] = value[:RADIUS]
            natural[: 192 - RADIUS, :] = value[RADIUS:]
        else:
            natural[192 * block - RADIUS : 192 * block - RADIUS + 192, :] = value
    for q in range(SUB):
        expo[q] = natural[pl.ds(q, CELLS, stride=SUB), :]
    place = place_lanes()
    stacks = []
    for s in range(SLOPES):
        factor = math.exp(0.64 * (s - 2))
        mean = jnp.zeros((CELLS, HEIGHT), F32)
        slant = jnp.zeros((CELLS, HEIGHT), F32)
        for q in range(SUB):
            fill = 1.0 / (1.0 + factor * expo[q])
            mean = mean + fill
            slant = slant + (q - 3.5) * fill
        stacks += [mean, mean * place, slant]
    stacks.append(jnp.zeros((SUB, HEIGHT), F32))
    rows = jnp.concatenate(parts_of(jnp.concatenate(stacks, axis=0), 2), axis=1)
    base = ((iota((256, 256), 0) % 128) // SUB == iota((256, 256), 1) % 16).astype(F32).astype(BF)
    pooled[...] = dot(rows, base) * (1.0 / 64.0)


def backward_body(expo, pooled, got, out, turned, to_near, to_far, natural):
    half = iota((1, 128), 1) < 64

    def pair(a, b):
        return jnp.where(half, a, b)

    def line(row):
        value = [got[g, row : row + 1, :] for g in range(4)]
        return jnp.concatenate([pair(value[0], value[1]), pair(value[2], value[3])], axis=1)

    level, eps_one, eps_two = (line(216), line(217), line(218))
    comps = []
    for slab in range(3):
        value = [got[g, 72 * slab : 72 * slab + 72, :] for g in range(4)]
        swapped = [pltpu.roll(v, 64, 1) for v in value]
        comps.append(jnp.concatenate([pair(value[0], swapped[1]), pair(value[2], swapped[3])], axis=1))
        comps.append(jnp.concatenate([pair(swapped[0], value[1]), pair(swapped[2], value[3])], axis=1))
    cxx, cyy, czz, cxy, cxz, cyz = comps
    frac = jnp.zeros((CELLS, 256), F32)
    grad_x = jnp.zeros((CELLS, 256), F32)
    grad_y = jnp.zeros((CELLS, 256), F32)
    masks = []
    for s in range(SLOPES):
        mask = level == float(s)
        masks.append(mask)
        frac = jnp.where(mask, pooled[216 * s : 216 * s + 72, :], frac)
        grad_x = jnp.where(mask, pooled[216 * s + 72 : 216 * s + 144, :], grad_x)
        grad_y = jnp.where(mask, pooled[216 * s + 144 : 216 * s + 216, :], grad_y)
    lift = 0.2 * (1.0 + level)
    slope_mean = eps_one - eps_two
    inv_two = 1.0 / eps_two
    slope_inv = 1.0 / eps_one - inv_two
    mean_eps = eps_two + frac * slope_mean
    harmonic = 1.0 / (inv_two + frac * slope_inv)
    inv_norm = 1.0 / (grad_x * grad_x + grad_y * grad_y + lift * lift)
    weight = (harmonic - mean_eps) * inv_norm
    along_x = cxx * grad_x + cxy * grad_y + cxz * lift
    along_y = cyy * grad_y + cyz * lift
    quad = grad_x * along_x + grad_y * along_y + czz * (lift * lift)
    trace = cxx + cyy + czz
    d_frac = trace * slope_mean - quad * inv_norm * (harmonic * harmonic * slope_inv + slope_mean)
    shared = 2.0 * inv_norm * quad
    d_x = weight * (along_x + cxx * grad_x - grad_x * shared)
    d_y = weight * (along_y + cyy * grad_y + cxy * grad_x - grad_y * shared)
    stack = jnp.concatenate([d_frac, d_x, d_y, jnp.zeros((SUB, 256), F32)], axis=0) * 0.5
    high, low = parts_of(stack, 2)
    spread = (iota((256, HEIGHT), 0) % 16 == iota((256, HEIGHT), 1) // SUB).astype(F32).astype(BF)
    place = place_lanes()
    flat, tilt = ([], [])
    for mask in masks:
        keep = jnp.where(mask, 1.0, 0.0).astype(BF)
        both = dot(high * keep, spread) + dot(low * keep, spread)
        flat.append(both[:72] + place * both[72:144])
        tilt.append(both[144:216])
    for q in range(SUB):
        total = jnp.zeros((CELLS, HEIGHT), F32)
        for s in range(SLOPES):
            scaled = math.exp(0.64 * (s - 2)) * expo[q]
            fill = 1.0 / (1.0 + scaled)
            total = total + (fill * fill * scaled) * (flat[s] + (q - 3.5) * tilt[s])
        natural[pl.ds(q, CELLS, stride=SUB), :] = total
    out[...] = natural[:WIDTH, :].T
    matrix = band(192, 256)
    pieces = []
    for block in range(3):
        count = 192 if block < 2 else 128
        if block == 0:
            window = jnp.concatenate([natural[WIDTH + RADIUS : WIDE, :], natural[:224, :]], axis=0)
        else:
            window = natural[192 * block - RADIUS : 192 * block + count + RADIUS, :]
        wide = dot(matrix[:count, : count + 64], jnp.concatenate(parts_of(window, 2), axis=1))
        pieces.append((wide[:, :128] + wide[:, 128:]) * SCALE)
    result = jnp.concatenate(pieces, axis=0).T
    turned[...] = result
    to_near[...], to_far[...] = sides("xy", result[:RADIUS], result[HEIGHT - RADIUS :])


def last_body(near, own, far, out):
    before, after = sides("xy", near[...], far[...])
    padded = jnp.concatenate([before, own[...], after], axis=0)
    matrix = band(HEIGHT, HEIGHT + 2 * RADIUS)
    high, low = parts_of(padded, 2)
    out[...] = (dot(matrix, high) + dot(matrix, low)) * SCALE


def swap(near, far, axis):
    count = lax.axis_size(axis)

    def pairs(start):
        return [p for i in range(start, count - 1, 2) for p in ((i, i + 1), (i + 1, i))]

    far = lax.ppermute(far, axis, pairs(1))
    near = lax.ppermute(near, axis, pairs(0))
    return (near, far)


def edges_body(density, near, far, sems):
    first = jnp.where(odd("xy"), 0, HEIGHT - RADIUS)
    second = HEIGHT - RADIUS - first
    copies = [
        pltpu.make_async_copy(density.at[pl.ds(pl.multiple_of(start, RADIUS), RADIUS)], target, sems.at[index])
        for index, (start, target) in enumerate([(first, near), (second, far)])
    ]
    for copy in copies:
        copy.start()
    for copy in copies:
        copy.wait()


def steps(density, cotangent, slope, layer_block, block_eps):
    near, far = pl.pallas_call(
        edges_body,
        name="edges",
        out_shape=[jax.ShapeDtypeStruct((RADIUS, WIDTH), F32)] * 2,
        in_specs=[pl.BlockSpec(memory_space=pltpu.HBM)],
        out_specs=[VMEM] * 2,
        scratch_shapes=[pltpu.SemaphoreType.DMA((2,))],
        compiler_params=pltpu.CompilerParams(vmem_limit_bytes=60 * 1024 * 1024),
        cost_estimate=pl.CostEstimate(flops=10**5, bytes_accessed=10**6, transcendentals=0),
    )(density)
    near, far = swap(near, far, "xy")
    (send,) = pl.pallas_call(
        pack_body,
        name="pack",
        out_shape=[jax.ShapeDtypeStruct((4, ROWS, 128), F32)],
        in_specs=[pl.BlockSpec(memory_space=pltpu.HBM)] * 4,
        out_specs=[VMEM],
        scratch_shapes=[
            pltpu.SMEM((4,), jnp.int32),
            pltpu.SMEM((4,), jnp.int32),
            pltpu.SMEM((2, 4), F32),
            pltpu.VMEM((384, 256), F32),
            pltpu.SemaphoreType.DMA((6,)),
        ],
        compiler_params=pltpu.CompilerParams(vmem_limit_bytes=60 * 1024 * 1024),
        cost_estimate=pl.CostEstimate(flops=10**6, bytes_accessed=10**6, transcendentals=0),
    )(slope, layer_block, block_eps.T, cotangent.reshape(384, 256))
    got = lax.all_to_all(send, "gz", 0, 0, tiled=True)
    across, near, far = (
        *call(rows_body, [(WIDTH, HEIGHT), (64, HEIGHT), (64, HEIGHT)], [], 10**8, 10**6, near, density, far),
    )
    near, far = swap(near, far, "gz")
    expo, pooled = call(forward_body, [(SUB, CELLS, HEIGHT), (1088, 256)], [(WIDE, HEIGHT)], 10**8, 2 * 10**6, near, across, far)
    own, turned, near, far = call(
        backward_body, [(HEIGHT, WIDTH), (HEIGHT, WIDTH), (RADIUS, WIDTH), (RADIUS, WIDTH)], [(WIDE, HEIGHT)], 10**8, 3 * 10**6, expo, pooled, got
    )
    near, far = swap(near, far, "xy")
    (result,) = call(last_body, [(HEIGHT, WIDTH)], [], 10**8, 10**6, near, turned, far)
    return (own, result)


def solution(mesh):
    return jax.shard_map(
        steps,
        mesh=mesh,
        in_specs=(P("xy", "gz"), P(None, "gz", "xy", None), P("gz"), P("gz"), P()),
        out_specs=(P("xy", "gz"), P("xy", "gz")),
        check_vma=False,
    )
```

```python
import math

import jax
import jax.numpy as jnp
from jax import lax
from jax.experimental import pallas as pl
from jax.experimental.pallas import tpu as pltpu
from jax.sharding import PartitionSpec as P

SUB = 8
RADIUS = 32
SLOPES = 5
SCALE = 1.0 / float((RADIUS + 1) ** 2)
BF = jnp.bfloat16
F32 = jnp.float32
VMEM = pl.BlockSpec(memory_space=pltpu.VMEM)
SMEM = pl.BlockSpec(memory_space=pltpu.SMEM)
HBM = pl.BlockSpec(memory_space=pltpu.HBM)
LIMIT = 24 << 20

HEIGHT = 128
WIDTH = 512
WIDE = WIDTH + 2 * RADIUS
CELLS = WIDE // SUB
ROWS = 224


def iota(shape, dim):
    return lax.broadcasted_iota(jnp.int32, shape, dim)


def parts_of(value, count):
    parts = []
    for index in range(count):
        part = value.astype(BF)
        parts.append(part)
        if index + 1 < count:
            value = value - part.astype(F32)
    return parts


def band(rows, cols):
    offset = iota((rows, cols), 1) - iota((rows, cols), 0) - RADIUS
    return jnp.maximum(RADIUS + 1 - jnp.abs(offset), 0).astype(F32).astype(BF)


def dot(a, b):
    return jnp.dot(a, b, preferred_element_type=F32)


def place_lanes():
    return (iota((1, HEIGHT), 1) % SUB).astype(F32) - 3.5


def call(body, outs, scratch, flops, moved, *args, smem=()):
    return pl.pallas_call(
        body,
        out_shape=[jax.ShapeDtypeStruct(shape, F32) for shape in outs],
        in_specs=[SMEM if index in smem else VMEM for index in range(len(args))],
        out_specs=[VMEM for _ in outs],
        scratch_shapes=[pltpu.VMEM(shape, F32) for shape in scratch],
        compiler_params=pltpu.CompilerParams(vmem_limit_bytes=LIMIT),
        cost_estimate=pl.CostEstimate(flops=flops, bytes_accessed=moved, transcendentals=0),
    )(*args)


def pack_body(slope_hbm, block_hbm, eps_hbm, cot_hbm, send_hbm, slope, block, eps, cot, send, sems):
    small = [
        pltpu.make_async_copy(source, target, sems.at[3 + index])
        for index, (source, target) in enumerate([(slope_hbm, slope), (block_hbm, block), (eps_hbm, eps)])
    ]
    slabs = [
        pltpu.make_async_copy(cot_hbm.at[pl.ds(128 * slab, 128)], cot.at[pl.ds(128 * slab, 128)], sems.at[slab])
        for slab in range(3)
    ]
    for copy in slabs + small:
        copy.start()
    low = iota((SUB, HEIGHT), 0) < 4
    zero = jnp.zeros((SUB, HEIGHT), F32)
    outs = []

    def put(first, rows):
        copy = pltpu.make_async_copy(
            send.at[:, pl.ds(first, rows)], send_hbm.at[:, pl.ds(first, rows)], sems.at[6 + len(outs)]
        )
        copy.start()
        outs.append(copy)

    for slab in range(3):
        slabs[slab].wait()
        turned = cot[slab * 128 : slab * 128 + 128, :].T
        for owner in range(4):
            first, base = (64 * owner, 72 * slab)
            send[owner, base : base + 64, :] = turned[first : first + 64]
            after = zero if owner == 3 else turned[first + 64 : first + 72]
            before = zero if owner == 0 else turned[first - 8 : first]
            send[owner, base + 64 : base + 72, :] = jnp.where(low, after, before)
        if slab < 2:
            put(72 * slab, 72)
    for copy in small:
        copy.wait()
    layer = (iota((SUB, HEIGHT), 1) % 64) // 16
    row = iota((SUB, HEIGHT), 0)
    table = zero
    for index in range(4):
        one = eps[0, block[index]]
        two = eps[1, block[index]]
        level = slope[index].astype(F32)
        column = jnp.where(row == 0, level, jnp.where(row == 1, one, jnp.where(row == 2, two, 0.0)))
        table = jnp.where(layer == index, column, table)
    for owner in range(4):
        send[owner, 216:224, :] = table
    put(144, 80)
    for copy in outs:
        copy.wait()


def odd(axis):
    return lax.rem(lax.axis_index(axis), 2) == 1


def sides(axis, near, far):
    return (jnp.where(odd(axis), near, far), jnp.where(odd(axis), far, near))


def low_lanes():
    return iota((1, 128), 1) < 64


def columns_body(own, to_near, to_far, rows_near, rows_far):
    begin, end = (own[:, :128], own[:, WIDTH - 128 :])
    first = jnp.where(low_lanes(), begin[:64], pltpu.roll(begin[64:], 64, 1))
    last = jnp.where(low_lanes(), pltpu.roll(end[:64], 64, 1), end[64:])
    to_near[...], to_far[...] = sides("gz", first, last)
    rows_near[...], rows_far[...] = sides("xy", own[:RADIUS], own[HEIGHT - RADIUS :])


def edges_body(near, far, rows_near, rows_far, halo, to_near, to_far):
    before, after = sides("gz", near[...], far[...])
    halo[:64] = jnp.where(low_lanes(), after, pltpu.roll(before, 64, 1))
    halo[64:] = jnp.where(low_lanes(), pltpu.roll(after, 64, 1), before)
    first, last = (slice(0, RADIUS), slice(HEIGHT - RADIUS, HEIGHT))
    to_near[:, :WIDTH] = rows_near[...]
    to_far[:, :WIDTH] = rows_far[...]
    to_near[:, WIDTH:], to_far[:, WIDTH:] = sides("xy", halo[first, :], halo[last, :])


def forward_body(near, own, halo, far, slopes, pooled, natural):
    before, after = sides("xy", near[...], far[...])
    middle = jnp.concatenate([own[...], halo[...]], axis=1)
    padded = jnp.concatenate([before, middle, after], axis=0)
    matrix = band(HEIGHT, HEIGHT + 2 * RADIUS)
    total = None
    for part in parts_of(padded, 3):
        term = dot(matrix, part)
        total = term if total is None else total + term
    turned = (total * SCALE).T
    padded = jnp.concatenate([turned[WIDTH + 64 :], turned[: WIDTH + 64]], axis=0)
    padded = jnp.concatenate(parts_of(padded, 3), axis=1)
    matrix = band(192, 256)
    for block in range(3):
        wide = dot(matrix, padded[192 * block : 192 * block + 256])
        field = (wide[:, :128] + wide[:, 128:256] + wide[:, 256:]) * SCALE
        value = jnp.exp(16.0 - 32.0 * field)
        if block == 0:
            natural[WIDTH + RADIUS : WIDE, :] = value[:RADIUS]
            natural[: 192 - RADIUS, :] = value[RADIUS:]
        else:
            natural[192 * block - RADIUS : 192 * block - RADIUS + 192, :] = value
    expo = [natural[pl.ds(q, CELLS, stride=SUB), :] for q in range(SUB)]
    place = place_lanes()
    stacks = []
    for s in range(SLOPES):
        factor = math.exp(0.64 * (s - 2))
        mean = jnp.zeros((CELLS, HEIGHT), F32)
        slant = jnp.zeros((CELLS, HEIGHT), F32)
        for q in range(SUB):
            scaled = factor * expo[q]
            fill = 1.0 / (1.0 + scaled)
            slopes[s, q] = fill * fill * scaled
            mean = mean + fill
            slant = slant + (q - 3.5) * fill
        stacks += [mean, mean * place, slant]
    stacks.append(jnp.zeros((SUB, HEIGHT), F32))
    rows = jnp.concatenate(parts_of(jnp.concatenate(stacks, axis=0), 2), axis=1)
    base = ((iota((256, 256), 0) % 128) // SUB == iota((256, 256), 1) % 16).astype(F32).astype(BF)
    pooled[...] = dot(rows, base) * (1.0 / 64.0)


def backward_body(slopes, pooled, got, out, turned, to_near, to_far, natural):
    half = low_lanes()

    def pair(a, b):
        return jnp.where(half, a, b)

    def line(row):
        value = [got[g, row : row + 1, :] for g in range(4)]
        return jnp.concatenate([pair(value[0], value[1]), pair(value[2], value[3])], axis=1)

    level, eps_one, eps_two = (line(216), line(217), line(218))
    comps = []
    for slab in range(3):
        value = [got[g, 72 * slab : 72 * slab + 72, :] for g in range(4)]
        swapped = [pltpu.roll(v, 64, 1) for v in value]
        comps.append(jnp.concatenate([pair(value[0], swapped[1]), pair(value[2], swapped[3])], axis=1))
        comps.append(jnp.concatenate([pair(swapped[0], value[1]), pair(swapped[2], value[3])], axis=1))
    cxx, cyy, czz, cxy, cxz, cyz = comps
    frac = jnp.zeros((CELLS, 256), F32)
    grad_x = jnp.zeros((CELLS, 256), F32)
    grad_y = jnp.zeros((CELLS, 256), F32)
    masks = []
    for s in range(SLOPES):
        mask = level == float(s)
        masks.append(mask)
        frac = jnp.where(mask, pooled[216 * s : 216 * s + 72, :], frac)
        grad_x = jnp.where(mask, pooled[216 * s + 72 : 216 * s + 144, :], grad_x)
        grad_y = jnp.where(mask, pooled[216 * s + 144 : 216 * s + 216, :], grad_y)
    lift = 0.2 * (1.0 + level)
    slope_mean = eps_one - eps_two
    inv_two = 1.0 / eps_two
    slope_inv = 1.0 / eps_one - inv_two
    mean_eps = eps_two + frac * slope_mean
    harmonic = 1.0 / (inv_two + frac * slope_inv)
    inv_norm = 1.0 / (grad_x * grad_x + grad_y * grad_y + lift * lift)
    weight = (harmonic - mean_eps) * inv_norm
    along_x = cxx * grad_x + cxy * grad_y + cxz * lift
    along_y = cyy * grad_y + cyz * lift
    quad = grad_x * along_x + grad_y * along_y + czz * (lift * lift)
    trace = cxx + cyy + czz
    d_frac = trace * slope_mean - quad * inv_norm * (harmonic * harmonic * slope_inv + slope_mean)
    shared = 2.0 * inv_norm * quad
    d_x = weight * (along_x + cxx * grad_x - grad_x * shared)
    d_y = weight * (along_y + cyy * grad_y + cxy * grad_x - grad_y * shared)
    stack = jnp.concatenate([d_frac, d_x, d_y, jnp.zeros((SUB, 256), F32)], axis=0) * 0.5
    high, low = parts_of(stack, 2)
    spread = (iota((256, HEIGHT), 0) % 16 == iota((256, HEIGHT), 1) // SUB).astype(F32).astype(BF)
    place = place_lanes()
    flat, tilt = ([], [])
    for mask in masks:
        keep = jnp.where(mask, 1.0, 0.0).astype(BF)
        both = dot(high * keep, spread) + dot(low * keep, spread)
        flat.append(both[:72] + place * both[72:144])
        tilt.append(both[144:216])
    for q in range(SUB):
        total = jnp.zeros((CELLS, HEIGHT), F32)
        for s in range(SLOPES):
            total = total + slopes[s, q] * (flat[s] + (q - 3.5) * tilt[s])
        natural[pl.ds(q, CELLS, stride=SUB), :] = total
    out[...] = natural[:WIDTH, :]
    matrix = band(192, 256)
    pieces = []
    for block in range(3):
        count = 192 if block < 2 else 128
        if block == 0:
            window = jnp.concatenate([natural[WIDTH + RADIUS : WIDE, :], natural[:224, :]], axis=0)
        else:
            window = natural[192 * block - RADIUS : 192 * block + count + RADIUS, :]
        wide = dot(matrix[:count, : count + 64], jnp.concatenate(parts_of(window, 2), axis=1))
        pieces.append((wide[:, :128] + wide[:, 128:]) * SCALE)
    result = jnp.concatenate(pieces, axis=0).T
    turned[...] = result
    to_near[...], to_far[...] = sides("xy", result[:RADIUS], result[HEIGHT - RADIUS :])


def emit_body(grad, turned, out, result, partial, middle, sem):
    matrix = band(HEIGHT, HEIGHT + 2 * RADIUS)[:, RADIUS : RADIUS + HEIGHT]
    high, low = parts_of(turned[...], 2)
    total = (dot(matrix, high) + dot(matrix, low)) * SCALE
    middle[...] = total[RADIUS : HEIGHT - RADIUS]
    copy = pltpu.make_async_copy(middle, result.at[pl.ds(RADIUS, HEIGHT - 2 * RADIUS)], sem)
    copy.start()
    partial[:RADIUS] = total[:RADIUS]
    partial[RADIUS:] = total[HEIGHT - RADIUS :]
    out[...] = grad[...].T
    copy.wait()


def last_body(near, partial, far, start, result, ends, sems):
    before, after = sides("xy", near[...], far[...])
    matrix = band(RADIUS, 3 * RADIUS)
    copies = []
    for index, (rows, weights) in enumerate([(before, matrix[:, :RADIUS]), (after, matrix[:, 2 * RADIUS :])]):
        high, low = parts_of(rows, 2)
        ends[index] = partial[RADIUS * index : RADIUS * (index + 1)] + (dot(weights, high) + dot(weights, low)) * SCALE
        where = result.at[pl.ds((HEIGHT - RADIUS) * index, RADIUS)]
        copies.append(pltpu.make_async_copy(ends.at[index], where, sems.at[index]))
        copies[-1].start()
    for copy in copies:
        copy.wait()


def swap(near, far, axis):
    count = lax.axis_size(axis)

    def pairs(start):
        return [p for i in range(start, count - 1, 2) for p in ((i, i + 1), (i + 1, i))]

    far = lax.ppermute(far, axis, pairs(1))
    near = lax.ppermute(near, axis, pairs(0))
    return (near, far)


def steps(density, cotangent, slope, layer_block, block_eps):
    shapes = [(64, 128), (64, 128), (RADIUS, WIDTH), (RADIUS, WIDTH)]
    near, far, *rows = call(columns_body, shapes, [], 10**5, 10**6, density)
    near, far = swap(near, far, "gz")
    (send,) = pl.pallas_call(
        pack_body,
        name="pack",
        out_shape=[jax.ShapeDtypeStruct((4, ROWS, 128), F32)],
        in_specs=[HBM] * 4,
        out_specs=[HBM],
        scratch_shapes=[
            pltpu.SMEM((4,), jnp.int32),
            pltpu.SMEM((4,), jnp.int32),
            pltpu.SMEM((2, 4), F32),
            pltpu.VMEM((384, 256), F32),
            pltpu.VMEM((4, ROWS, 128), F32),
            pltpu.SemaphoreType.DMA((9,)),
        ],
        compiler_params=pltpu.CompilerParams(vmem_limit_bytes=60 * 1024 * 1024),
        cost_estimate=pl.CostEstimate(flops=10**6, bytes_accessed=10**6, transcendentals=0),
    )(slope, layer_block, block_eps.T, cotangent.reshape(384, 256))
    got = lax.all_to_all(send, "gz", 0, 0, tiled=True)
    edges = [(HEIGHT, 128), (RADIUS, WIDTH + 128), (RADIUS, WIDTH + 128)]
    halo, near, far = call(edges_body, edges, [], 10**5, 10**6, near, far, *rows)
    near, far = swap(near, far, "xy")
    slopes, pooled = call(
        forward_body,
        [(SLOPES, SUB, CELLS, HEIGHT), (1088, 256)],
        [(WIDE, HEIGHT)],
        10**8,
        2 * 10**6,
        near,
        density,
        halo,
        far,
    )
    shapes = [(WIDTH, HEIGHT), (HEIGHT, WIDTH), (RADIUS, WIDTH), (RADIUS, WIDTH)]
    grad, turned, near, far = call(backward_body, shapes, [(WIDE, HEIGHT)], 10**8, 3 * 10**6, slopes, pooled, got)
    near, far = swap(near, far, "xy")
    whole = jax.ShapeDtypeStruct((HEIGHT, WIDTH), F32)
    own, result, partial = pl.pallas_call(
        emit_body,
        name="emit",
        out_shape=[whole, whole, jax.ShapeDtypeStruct((2 * RADIUS, WIDTH), F32)],
        in_specs=[VMEM] * 2,
        out_specs=[VMEM, HBM, VMEM],
        scratch_shapes=[pltpu.VMEM((HEIGHT - 2 * RADIUS, WIDTH), F32), pltpu.SemaphoreType.DMA],
        compiler_params=pltpu.CompilerParams(vmem_limit_bytes=LIMIT),
        cost_estimate=pl.CostEstimate(flops=10**8, bytes_accessed=10**6, transcendentals=0),
    )(grad, turned)
    result = pl.pallas_call(
        last_body,
        name="last",
        out_shape=whole,
        in_specs=[VMEM] * 3 + [HBM],
        out_specs=HBM,
        scratch_shapes=[pltpu.VMEM((2, RADIUS, WIDTH), F32), pltpu.SemaphoreType.DMA((2,))],
        input_output_aliases={3: 0},
        compiler_params=pltpu.CompilerParams(vmem_limit_bytes=LIMIT),
        cost_estimate=pl.CostEstimate(flops=10**7, bytes_accessed=10**6, transcendentals=0),
    )(near, partial, far, result)
    return (own, result)


def solution(mesh):
    return jax.shard_map(
        steps,
        mesh=mesh,
        in_specs=(P("xy", "gz"), P(None, "gz", "xy", None), P("gz"), P("gz"), P()),
        out_specs=(P("xy", "gz"), P("xy", "gz")),
        check_vma=False,
    )
```

```python
import math

import jax
import jax.numpy as jnp
from jax import lax
from jax.experimental import pallas as pl
from jax.experimental.pallas import tpu as pltpu
from jax.sharding import PartitionSpec as P

SUB = 8
RADIUS = 32
SLOPES = 5
SCALE = 1.0 / float((RADIUS + 1) ** 2)
BF = jnp.bfloat16
F32 = jnp.float32
VMEM = pl.BlockSpec(memory_space=pltpu.VMEM)
SMEM = pl.BlockSpec(memory_space=pltpu.SMEM)
HBM = pl.BlockSpec(memory_space=pltpu.HBM)
LIMIT = 24 << 20

HEIGHT = 128
WIDTH = 512
WIDE = WIDTH + 2 * RADIUS
CELLS = WIDE // SUB
ROWS = 224


def iota(shape, dim):
    return lax.broadcasted_iota(jnp.int32, shape, dim)


def parts_of(value, count):
    parts = []
    for index in range(count):
        part = value.astype(BF)
        parts.append(part)
        if index + 1 < count:
            value = value - part.astype(F32)
    return parts


def band(rows, cols):
    offset = iota((rows, cols), 1) - iota((rows, cols), 0) - RADIUS
    return jnp.maximum(RADIUS + 1 - jnp.abs(offset), 0).astype(F32).astype(BF)


def dot(a, b):
    return jnp.dot(a, b, preferred_element_type=F32)


def place_lanes():
    return (iota((1, HEIGHT), 1) % SUB).astype(F32) - 3.5


def call(body, outs, scratch, flops, moved, *args, smem=()):
    return pl.pallas_call(
        body,
        out_shape=[jax.ShapeDtypeStruct(shape, F32) for shape in outs],
        in_specs=[SMEM if index in smem else VMEM for index in range(len(args))],
        out_specs=[VMEM for _ in outs],
        scratch_shapes=[pltpu.VMEM(shape, F32) for shape in scratch],
        compiler_params=pltpu.CompilerParams(vmem_limit_bytes=LIMIT),
        cost_estimate=pl.CostEstimate(flops=flops, bytes_accessed=moved, transcendentals=0),
    )(*args)


def pack_body(slope_hbm, block_hbm, eps_hbm, cot_hbm, send_hbm, slope, block, eps, cot, send, sems):
    small = [
        pltpu.make_async_copy(source, target, sems.at[3 + index])
        for index, (source, target) in enumerate([(slope_hbm, slope), (block_hbm, block), (eps_hbm, eps)])
    ]
    slabs = [
        pltpu.make_async_copy(cot_hbm.at[pl.ds(128 * slab, 128)], cot.at[pl.ds(128 * slab, 128)], sems.at[slab])
        for slab in range(3)
    ]
    for copy in slabs + small:
        copy.start()
    low = iota((SUB, HEIGHT), 0) < 4
    zero = jnp.zeros((SUB, HEIGHT), F32)
    outs = []

    def put(first, rows):
        copy = pltpu.make_async_copy(
            send.at[:, pl.ds(first, rows)], send_hbm.at[:, pl.ds(first, rows)], sems.at[6 + len(outs)]
        )
        copy.start()
        outs.append(copy)

    for slab in range(3):
        slabs[slab].wait()
        turned = cot[slab * 128 : slab * 128 + 128, :].T
        for owner in range(4):
            first, base = (64 * owner, 72 * slab)
            send[owner, base : base + 64, :] = turned[first : first + 64]
            after = zero if owner == 3 else turned[first + 64 : first + 72]
            before = zero if owner == 0 else turned[first - 8 : first]
            send[owner, base + 64 : base + 72, :] = jnp.where(low, after, before)
        if slab < 2:
            put(72 * slab, 72)
    for copy in small:
        copy.wait()
    layer = (iota((SUB, HEIGHT), 1) % 64) // 16
    row = iota((SUB, HEIGHT), 0)
    table = zero
    for index in range(4):
        one = eps[0, block[index]]
        two = eps[1, block[index]]
        level = slope[index].astype(F32)
        column = jnp.where(row == 0, level, jnp.where(row == 1, one, jnp.where(row == 2, two, 0.0)))
        table = jnp.where(layer == index, column, table)
    for owner in range(4):
        send[owner, 216:224, :] = table
    put(144, 80)
    for copy in outs:
        copy.wait()


def odd(axis):
    return lax.rem(lax.axis_index(axis), 2) == 1


def sides(axis, near, far):
    return (jnp.where(odd(axis), near, far), jnp.where(odd(axis), far, near))


def low_lanes():
    return iota((1, 128), 1) < 64


def columns_body(own, to_near, to_far, rows_near, rows_far):
    begin, end = (own[:, :128], own[:, WIDTH - 128 :])
    first = jnp.where(low_lanes(), begin[:64], pltpu.roll(begin[64:], 64, 1))
    last = jnp.where(low_lanes(), pltpu.roll(end[:64], 64, 1), end[64:])
    to_near[...], to_far[...] = sides("gz", first, last)
    rows_near[...], rows_far[...] = sides("xy", own[:RADIUS], own[HEIGHT - RADIUS :])


def edges_body(near, far, rows_near, rows_far, halo, to_near, to_far):
    before, after = sides("gz", near[...], far[...])
    halo[:64] = jnp.where(low_lanes(), after, pltpu.roll(before, 64, 1))
    halo[64:] = jnp.where(low_lanes(), pltpu.roll(after, 64, 1), before)
    first, last = (slice(0, RADIUS), slice(HEIGHT - RADIUS, HEIGHT))
    to_near[:, :WIDTH] = rows_near[...]
    to_far[:, :WIDTH] = rows_far[...]
    to_near[:, WIDTH:], to_far[:, WIDTH:] = sides("xy", halo[first, :], halo[last, :])


def forward_body(own, halo, near, down, up, slopes, pooled, natural):
    before, after = sides("xy", near[...], jnp.where(odd("xy"), up[...], down[...]))
    middle = jnp.concatenate([own[...], halo[...]], axis=1)
    padded = jnp.concatenate([before, middle, after], axis=0)
    matrix = band(HEIGHT, HEIGHT + 2 * RADIUS)
    total = None
    for part in parts_of(padded, 3):
        term = dot(matrix, part)
        total = term if total is None else total + term
    turned = (total * SCALE).T
    padded = jnp.concatenate([turned[WIDTH + 64 :], turned[: WIDTH + 64]], axis=0)
    padded = jnp.concatenate(parts_of(padded, 3), axis=1)
    matrix = band(192, 256)
    for block in range(3):
        wide = dot(matrix, padded[192 * block : 192 * block + 256])
        field = (wide[:, :128] + wide[:, 128:256] + wide[:, 256:]) * SCALE
        value = jnp.exp(16.0 - 32.0 * field)
        if block == 0:
            natural[WIDTH + RADIUS : WIDE, :] = value[:RADIUS]
            natural[: 192 - RADIUS, :] = value[RADIUS:]
        else:
            natural[192 * block - RADIUS : 192 * block - RADIUS + 192, :] = value
    expo = [natural[pl.ds(q, CELLS, stride=SUB), :] for q in range(SUB)]
    place = place_lanes()
    stacks = []
    for s in range(SLOPES):
        factor = math.exp(0.64 * (s - 2))
        mean = jnp.zeros((CELLS, HEIGHT), F32)
        slant = jnp.zeros((CELLS, HEIGHT), F32)
        for q in range(SUB):
            scaled = factor * expo[q]
            fill = 1.0 / (1.0 + scaled)
            slopes[s, q] = fill * fill * scaled
            mean = mean + fill
            slant = slant + (q - 3.5) * fill
        stacks += [mean, mean * place, slant]
    stacks.append(jnp.zeros((SUB, HEIGHT), F32))
    rows = jnp.concatenate(parts_of(jnp.concatenate(stacks, axis=0), 2), axis=1)
    base = ((iota((256, 256), 0) % 128) // SUB == iota((256, 256), 1) % 16).astype(F32).astype(BF)
    pooled[...] = dot(rows, base) * (1.0 / 64.0)


def backward_body(slopes, pooled, got, out, turned, to_near, to_far, natural):
    half = low_lanes()

    def pair(a, b):
        return jnp.where(half, a, b)

    def line(row):
        value = [got[g, row : row + 1, :] for g in range(4)]
        return jnp.concatenate([pair(value[0], value[1]), pair(value[2], value[3])], axis=1)

    level, eps_one, eps_two = (line(216), line(217), line(218))
    comps = []
    for slab in range(3):
        value = [got[g, 72 * slab : 72 * slab + 72, :] for g in range(4)]
        swapped = [pltpu.roll(v, 64, 1) for v in value]
        comps.append(jnp.concatenate([pair(value[0], swapped[1]), pair(value[2], swapped[3])], axis=1))
        comps.append(jnp.concatenate([pair(swapped[0], value[1]), pair(swapped[2], value[3])], axis=1))
    cxx, cyy, czz, cxy, cxz, cyz = comps
    frac = jnp.zeros((CELLS, 256), F32)
    grad_x = jnp.zeros((CELLS, 256), F32)
    grad_y = jnp.zeros((CELLS, 256), F32)
    masks = []
    for s in range(SLOPES):
        mask = level == float(s)
        masks.append(mask)
        frac = jnp.where(mask, pooled[216 * s : 216 * s + 72, :], frac)
        grad_x = jnp.where(mask, pooled[216 * s + 72 : 216 * s + 144, :], grad_x)
        grad_y = jnp.where(mask, pooled[216 * s + 144 : 216 * s + 216, :], grad_y)
    lift = 0.2 * (1.0 + level)
    slope_mean = eps_one - eps_two
    inv_two = 1.0 / eps_two
    slope_inv = 1.0 / eps_one - inv_two
    mean_eps = eps_two + frac * slope_mean
    harmonic = 1.0 / (inv_two + frac * slope_inv)
    inv_norm = 1.0 / (grad_x * grad_x + grad_y * grad_y + lift * lift)
    weight = (harmonic - mean_eps) * inv_norm
    along_x = cxx * grad_x + cxy * grad_y + cxz * lift
    along_y = cyy * grad_y + cyz * lift
    quad = grad_x * along_x + grad_y * along_y + czz * (lift * lift)
    trace = cxx + cyy + czz
    d_frac = trace * slope_mean - quad * inv_norm * (harmonic * harmonic * slope_inv + slope_mean)
    shared = 2.0 * inv_norm * quad
    d_x = weight * (along_x + cxx * grad_x - grad_x * shared)
    d_y = weight * (along_y + cyy * grad_y + cxy * grad_x - grad_y * shared)
    stack = jnp.concatenate([d_frac, d_x, d_y, jnp.zeros((SUB, 256), F32)], axis=0) * 0.5
    high, low = parts_of(stack, 2)
    spread = (iota((256, HEIGHT), 0) % 16 == iota((256, HEIGHT), 1) // SUB).astype(F32).astype(BF)
    place = place_lanes()
    flat, tilt = ([], [])
    for mask in masks:
        keep = jnp.where(mask, 1.0, 0.0).astype(BF)
        both = dot(high * keep, spread) + dot(low * keep, spread)
        flat.append(both[:72] + place * both[72:144])
        tilt.append(both[144:216])
    for q in range(SUB):
        total = jnp.zeros((CELLS, HEIGHT), F32)
        for s in range(SLOPES):
            total = total + slopes[s, q] * (flat[s] + (q - 3.5) * tilt[s])
        natural[pl.ds(q, CELLS, stride=SUB), :] = total
    out[...] = natural[:WIDTH, :]
    matrix = band(192, 256)
    pieces = []
    for block in range(3):
        count = 192 if block < 2 else 128
        if block == 0:
            window = jnp.concatenate([natural[WIDTH + RADIUS : WIDE, :], natural[:224, :]], axis=0)
        else:
            window = natural[192 * block - RADIUS : 192 * block + count + RADIUS, :]
        wide = dot(matrix[:count, : count + 64], jnp.concatenate(parts_of(window, 2), axis=1))
        pieces.append((wide[:, :128] + wide[:, 128:]) * SCALE)
    result = jnp.concatenate(pieces, axis=0).T
    turned[...] = result
    to_near[...], to_far[...] = sides("xy", result[:RADIUS], result[HEIGHT - RADIUS :])


def emit_body(grad, turned, out, result, partial, whole, middle, sems):
    whole[...] = grad[...].T
    copies = [pltpu.make_async_copy(whole, out, sems.at[0])]
    copies[0].start()
    matrix = band(HEIGHT, HEIGHT + 2 * RADIUS)[:, RADIUS : RADIUS + HEIGHT]
    high, low = parts_of(turned[...], 2)
    total = (dot(matrix, high) + dot(matrix, low)) * SCALE
    middle[...] = total[RADIUS : HEIGHT - RADIUS]
    copies.append(pltpu.make_async_copy(middle, result.at[pl.ds(RADIUS, HEIGHT - 2 * RADIUS)], sems.at[1]))
    copies[1].start()
    partial[:RADIUS] = total[:RADIUS]
    partial[RADIUS:] = total[HEIGHT - RADIUS :]
    for copy in copies:
        copy.wait()


def last_body(near, far, partial, start, result, ends, sems):
    before, after = sides("xy", near[...], far[...])
    matrix = band(RADIUS, 3 * RADIUS)
    copies = []
    for index, (rows, weights) in enumerate([(before, matrix[:, :RADIUS]), (after, matrix[:, 2 * RADIUS :])]):
        high, low = parts_of(rows, 2)
        ends[index] = partial[RADIUS * index : RADIUS * (index + 1)] + (dot(weights, high) + dot(weights, low)) * SCALE
        where = result.at[pl.ds((HEIGHT - RADIUS) * index, RADIUS)]
        copies.append(pltpu.make_async_copy(ends.at[index], where, sems.at[index]))
        copies[-1].start()
    for copy in copies:
        copy.wait()


def pairs(axis, start):
    return [(i, i + 1) for i in range(start, lax.axis_size(axis) - 1, 2)]


def back(steps):
    return [(j, i) for i, j in steps]


def swap(near, far, axis):
    inner, outer = (pairs(axis, 0), pairs(axis, 1))
    far = lax.ppermute(far, axis, outer + back(outer))
    return (lax.ppermute(near, axis, inner + back(inner)), far)


def steps(density, cotangent, slope, layer_block, block_eps):
    shapes = [(64, 128), (64, 128), (RADIUS, WIDTH), (RADIUS, WIDTH)]
    near, far, *rows = call(columns_body, shapes, [], 10**5, 10**6, density)
    near, far = swap(near, far, "gz")
    (send,) = pl.pallas_call(
        pack_body,
        name="pack",
        out_shape=[jax.ShapeDtypeStruct((4, ROWS, 128), F32)],
        in_specs=[HBM] * 4,
        out_specs=[HBM],
        scratch_shapes=[
            pltpu.SMEM((4,), jnp.int32),
            pltpu.SMEM((4,), jnp.int32),
            pltpu.SMEM((2, 4), F32),
            pltpu.VMEM((384, 256), F32),
            pltpu.VMEM((4, ROWS, 128), F32),
            pltpu.SemaphoreType.DMA((9,)),
        ],
        compiler_params=pltpu.CompilerParams(vmem_limit_bytes=60 * 1024 * 1024),
        cost_estimate=pl.CostEstimate(flops=10**6, bytes_accessed=10**6, transcendentals=0),
    )(slope, layer_block, block_eps.T, cotangent.reshape(384, 256))
    got = lax.all_to_all(send, "gz", 0, 0, tiled=True)
    edges = [(HEIGHT, 128), (RADIUS, WIDTH + 128), (RADIUS, WIDTH + 128)]
    halo, near, far = call(edges_body, edges, [], 10**5, 10**6, near, far, *rows)
    inner, outer = (pairs("xy", 0), pairs("xy", 1))
    down = lax.ppermute(far, "xy", outer)
    up = lax.ppermute(far, "xy", back(outer))
    near = lax.ppermute(near, "xy", inner + back(inner))
    slopes, pooled = call(
        forward_body,
        [(SLOPES, SUB, CELLS, HEIGHT), (1088, 256)],
        [(WIDE, HEIGHT)],
        10**8,
        2 * 10**6,
        density,
        halo,
        near,
        down,
        up,
    )
    shapes = [(WIDTH, HEIGHT), (HEIGHT, WIDTH), (RADIUS, WIDTH), (RADIUS, WIDTH)]
    grad, turned, near, far = call(backward_body, shapes, [(WIDE, HEIGHT)], 10**8, 3 * 10**6, slopes, pooled, got)
    near, far = swap(near, far, "xy")
    whole = jax.ShapeDtypeStruct((HEIGHT, WIDTH), F32)
    own, result, partial = pl.pallas_call(
        emit_body,
        name="emit",
        out_shape=[whole, whole, jax.ShapeDtypeStruct((2 * RADIUS, WIDTH), F32)],
        in_specs=[VMEM] * 2,
        out_specs=[HBM, HBM, VMEM],
        scratch_shapes=[
            pltpu.VMEM((HEIGHT, WIDTH), F32),
            pltpu.VMEM((HEIGHT - 2 * RADIUS, WIDTH), F32),
            pltpu.SemaphoreType.DMA((2,)),
        ],
        compiler_params=pltpu.CompilerParams(vmem_limit_bytes=LIMIT),
        cost_estimate=pl.CostEstimate(flops=10**8, bytes_accessed=10**6, transcendentals=0),
    )(grad, turned)
    result = pl.pallas_call(
        last_body,
        name="last",
        out_shape=whole,
        in_specs=[VMEM] * 3 + [HBM],
        out_specs=HBM,
        scratch_shapes=[pltpu.VMEM((2, RADIUS, WIDTH), F32), pltpu.SemaphoreType.DMA((2,))],
        input_output_aliases={3: 0},
        compiler_params=pltpu.CompilerParams(vmem_limit_bytes=LIMIT),
        cost_estimate=pl.CostEstimate(flops=10**7, bytes_accessed=10**6, transcendentals=0),
    )(near, far, partial, result)
    return (own, result)


def solution(mesh):
    return jax.shard_map(
        steps,
        mesh=mesh,
        in_specs=(P("xy", "gz"), P(None, "gz", "xy", None), P("gz"), P("gz"), P()),
        out_specs=(P("xy", "gz"), P("xy", "gz")),
        check_vma=False,
    )
```

```python
import math

import jax
import jax.numpy as jnp
from jax import lax
from jax.experimental import pallas as pl
from jax.experimental.pallas import tpu as pltpu
from jax.sharding import PartitionSpec as P

SUB = 8
RADIUS = 32
SLOPES = 5
SCALE = 1.0 / float((RADIUS + 1) ** 2)
BF = jnp.bfloat16
F32 = jnp.float32
VMEM = pl.BlockSpec(memory_space=pltpu.VMEM)
SMEM = pl.BlockSpec(memory_space=pltpu.SMEM)
HBM = pl.BlockSpec(memory_space=pltpu.HBM)
LIMIT = 24 << 20

HEIGHT = 128
WIDTH = 512
WIDE = WIDTH + 2 * RADIUS
CELLS = WIDE // SUB
ROWS = 224


def iota(shape, dim):
    return lax.broadcasted_iota(jnp.int32, shape, dim)


def parts_of(value, count):
    parts = []
    for index in range(count):
        part = value.astype(BF)
        parts.append(part)
        if index + 1 < count:
            value = value - part.astype(F32)
    return parts


def band(rows, cols):
    offset = iota((rows, cols), 1) - iota((rows, cols), 0) - RADIUS
    return jnp.maximum(RADIUS + 1 - jnp.abs(offset), 0).astype(F32).astype(BF)


def dot(a, b):
    return jnp.dot(a, b, preferred_element_type=F32)


def place_lanes():
    return (iota((1, HEIGHT), 1) % SUB).astype(F32) - 3.5


def call(body, outs, scratch, flops, moved, *args, smem=()):
    return pl.pallas_call(
        body,
        out_shape=[out if hasattr(out, "dtype") else jax.ShapeDtypeStruct(out, F32) for out in outs],
        in_specs=[SMEM if index in smem else VMEM for index in range(len(args))],
        out_specs=[VMEM for _ in outs],
        scratch_shapes=[pltpu.VMEM(shape, F32) for shape in scratch],
        compiler_params=pltpu.CompilerParams(vmem_limit_bytes=LIMIT),
        cost_estimate=pl.CostEstimate(flops=flops, bytes_accessed=moved, transcendentals=0),
    )(*args)


def pack_body(slope_hbm, block_hbm, eps_hbm, cot_hbm, send_hbm, slope, block, eps, cot, send, sems):
    small = [
        pltpu.make_async_copy(source, target, sems.at[3 + index])
        for index, (source, target) in enumerate([(slope_hbm, slope), (block_hbm, block), (eps_hbm, eps)])
    ]
    slabs = [
        pltpu.make_async_copy(cot_hbm.at[pl.ds(128 * slab, 128)], cot.at[pl.ds(128 * slab, 128)], sems.at[slab])
        for slab in range(3)
    ]
    for copy in slabs + small:
        copy.start()
    low = iota((SUB, HEIGHT), 0) < 4
    zero = jnp.zeros((SUB, HEIGHT), F32)
    outs = []

    def put(first, rows):
        copy = pltpu.make_async_copy(
            send.at[:, pl.ds(first, rows)], send_hbm.at[:, pl.ds(first, rows)], sems.at[6 + len(outs)]
        )
        copy.start()
        outs.append(copy)

    for slab in range(3):
        slabs[slab].wait()
        turned = cot[slab * 128 : slab * 128 + 128, :].T
        for owner in range(4):
            first, base = (64 * owner, 72 * slab)
            send[owner, base : base + 64, :] = turned[first : first + 64]
            after = zero if owner == 3 else turned[first + 64 : first + 72]
            before = zero if owner == 0 else turned[first - 8 : first]
            send[owner, base + 64 : base + 72, :] = jnp.where(low, after, before)
        if slab < 2:
            put(72 * slab, 72)
    for copy in small:
        copy.wait()
    layer = (iota((SUB, HEIGHT), 1) % 64) // 16
    row = iota((SUB, HEIGHT), 0)
    table = zero
    for index in range(4):
        one = eps[0, block[index]]
        two = eps[1, block[index]]
        level = slope[index].astype(F32)
        column = jnp.where(row == 0, level, jnp.where(row == 1, one, jnp.where(row == 2, two, 0.0)))
        table = jnp.where(layer == index, column, table)
    for owner in range(4):
        send[owner, 216:224, :] = table
    put(144, 80)
    for copy in outs:
        copy.wait()


def odd(axis):
    return lax.rem(lax.axis_index(axis), 2) == 1


def sides(axis, near, far):
    return (jnp.where(odd(axis), near, far), jnp.where(odd(axis), far, near))


def low_lanes():
    return iota((1, 128), 1) < 64


def columns_body(density, to_near, to_far, rows_near, rows_far, begin, end, sems):
    first = jnp.where(odd("xy"), 0, HEIGHT - RADIUS)
    moves = [
        (density.at[:, pl.ds(0, 128)], begin),
        (density.at[:, pl.ds(WIDTH - 128, 128)], end),
        (density.at[pl.ds(pl.multiple_of(first, RADIUS), RADIUS)], rows_near),
        (density.at[pl.ds(pl.multiple_of(HEIGHT - RADIUS - first, RADIUS), RADIUS)], rows_far),
    ]
    copies = [pltpu.make_async_copy(source, target, sems.at[index]) for index, (source, target) in enumerate(moves)]
    for copy in copies:
        copy.start()
    copies[0].wait()
    copies[1].wait()
    first = jnp.where(low_lanes(), begin[:64, :], pltpu.roll(begin[64:, :], 64, 1))
    last = jnp.where(low_lanes(), pltpu.roll(end[:64, :], 64, 1), end[64:, :])
    to_near[...], to_far[...] = sides("gz", first, last)
    copies[2].wait()
    copies[3].wait()


def edges_body(near, far, rows_near, rows_far, halo, to_near, to_far):
    before, after = sides("gz", near[...], far[...])
    halo[:64] = jnp.where(low_lanes(), after, pltpu.roll(before, 64, 1))
    halo[64:] = jnp.where(low_lanes(), pltpu.roll(after, 64, 1), before)
    first, last = (slice(0, RADIUS), slice(HEIGHT - RADIUS, HEIGHT))
    to_near[:, :WIDTH] = rows_near[...]
    to_far[:, :WIDTH] = rows_far[...]
    to_near[:, WIDTH:], to_far[:, WIDTH:] = sides("xy", halo[first, :], halo[last, :])


def prior_body(own, halo, start, across, ahead, plain, pool, spread):
    middle = jnp.concatenate([own[...], halo[...]], axis=1)
    matrix = band(HEIGHT, HEIGHT + 2 * RADIUS)[:, RADIUS : RADIUS + HEIGHT]
    total = None
    for part in parts_of(middle, 3):
        term = dot(matrix, part)
        total = term if total is None else total + term
    turned = total.T
    padded = jnp.concatenate([turned[WIDTH + 64 :], turned[: WIDTH + 64]], axis=0)
    padded = jnp.concatenate(parts_of(padded, 3), axis=1)
    matrix = band(192, 256)
    plain[...] = matrix
    for block in range(3):
        wide = dot(matrix, padded[192 * block : 192 * block + 256])
        keep(start, block, wide[:, :128] + wide[:, 128:256] + wide[:, 256:])
    offset = iota((384, 192), 0) - iota((384, 192), 1) - 3 * RADIUS
    across[...] = jnp.maximum(RADIUS + 1 - jnp.abs(offset), 0).astype(F32).astype(BF)
    row = iota((HEIGHT, 192), 1) % 64
    offset = row + jnp.where(row < RADIUS, -RADIUS, 3 * RADIUS) - iota((HEIGHT, 192), 0)
    ahead[...] = jnp.maximum(RADIUS + 1 - jnp.abs(offset), 0).astype(F32).astype(BF)
    base = (iota((128, 256), 0) // SUB == iota((128, 256), 1) % 16).astype(F32).astype(BF)
    pool[...] = jnp.concatenate([base, base], axis=0)
    spread[...] = (iota((256, HEIGHT), 0) % 16 == iota((256, HEIGHT), 1) // SUB).astype(F32).astype(BF)


def places(block):
    first = 192 * block - RADIUS
    return [(0, RADIUS, WIDTH + RADIUS), (RADIUS, 192, 0)] if block == 0 else [(0, 192, first)]


def keep(target, block, value):
    for begin, end, first in places(block):
        target[first : first + end - begin, :] = value[begin:end]


def forward(near, down, up, start, across, ahead, pool, slopes, pooled, natural):
    before, after = sides("xy", near[...], jnp.where(odd("xy"), up[...], down[...]))
    rows = jnp.concatenate(parts_of(jnp.concatenate([before, after], axis=0), 3), axis=0)
    windows = [jnp.concatenate([rows[:, WIDTH:], rows[:, :256]], axis=1), rows[:, 128:384], rows[:, 256:]]
    for block, window in enumerate(windows):
        weights = across[64:320, :] if block == 1 else across[...]
        wide = dot(window, weights)
        beside = parts_of(wide[:64] + wide[64:128] + wide[128:], 3)
        added = dot(ahead[...], jnp.concatenate(beside, axis=0)).T
        own = jnp.concatenate([start[first : first + end - begin, :] for begin, end, first in places(block)], axis=0)
        keep(natural, block, jnp.exp(16.0 - (32.0 * SCALE * SCALE) * (own + added)))
    expo = [natural[pl.ds(q, CELLS, stride=SUB), :] for q in range(SUB)]
    place = place_lanes()
    stacks = []
    for s in range(SLOPES):
        factor = math.exp(0.64 * (s - 2))
        mean, slant = (None, None)
        for q in range(SUB // 2):
            pair = []
            for row in (q, SUB - 1 - q):
                scaled = factor * expo[row]
                fill = 1.0 / (1.0 + scaled)
                slopes[s, row] = fill * fill * scaled
                pair.append(fill)
            both, apart = (pair[0] + pair[1], (3.5 - q) * (pair[1] - pair[0]))
            mean = both if mean is None else mean + both
            slant = apart if slant is None else slant + apart
        stacks += [mean, mean * place, slant]
    stacks.append(jnp.zeros((SUB, HEIGHT), F32))
    rows = jnp.concatenate(parts_of(jnp.concatenate(stacks, axis=0), 2), axis=1)
    pooled[...] = dot(rows, pool[...])


def adjoint_body(near, down, up, got, start, across, ahead, plain, pool, spread, out, turned, to_near, to_far, slopes, pooled, natural):
    forward(near, down, up, start, across, ahead, pool, slopes, pooled, natural)
    half = low_lanes()

    def pair(a, b):
        return jnp.where(half, a, b)

    def line(row):
        value = [got[g, row : row + 1, :] for g in range(4)]
        return jnp.concatenate([pair(value[0], value[1]), pair(value[2], value[3])], axis=1)

    level, eps_one, eps_two = (line(216), line(217), line(218))
    comps = []
    for slab in range(3):
        value = [got[g, 72 * slab : 72 * slab + 72, :] for g in range(4)]
        swapped = [pltpu.roll(v, 64, 1) for v in value]
        comps.append(jnp.concatenate([pair(value[0], swapped[1]), pair(value[2], swapped[3])], axis=1))
        comps.append(jnp.concatenate([pair(swapped[0], value[1]), pair(swapped[2], value[3])], axis=1))
    cxx, cyy, czz, cxy, cxz, cyz = comps
    frac = jnp.zeros((CELLS, 256), F32)
    grad_x = jnp.zeros((CELLS, 256), F32)
    grad_y = jnp.zeros((CELLS, 256), F32)
    masks = []
    for s in range(SLOPES):
        mask = level == float(s)
        masks.append(mask)
        frac = jnp.where(mask, pooled[216 * s : 216 * s + 72, :], frac)
        grad_x = jnp.where(mask, pooled[216 * s + 72 : 216 * s + 144, :], grad_x)
        grad_y = jnp.where(mask, pooled[216 * s + 144 : 216 * s + 216, :], grad_y)
    frac, grad_x, grad_y = (value * (1.0 / 64.0) for value in (frac, grad_x, grad_y))
    lift = 0.2 * (1.0 + level)
    slope_mean = eps_one - eps_two
    inv_two = 1.0 / eps_two
    slope_inv = 1.0 / eps_one - inv_two
    mean_eps = eps_two + frac * slope_mean
    harmonic = 1.0 / (inv_two + frac * slope_inv)
    inv_norm = 1.0 / (grad_x * grad_x + grad_y * grad_y + lift * lift)
    weight = (harmonic - mean_eps) * inv_norm
    along_x = cxx * grad_x + cxy * grad_y + cxz * lift
    along_y = cyy * grad_y + cyz * lift
    quad = grad_x * along_x + grad_y * along_y + czz * (lift * lift)
    trace = cxx + cyy + czz
    d_frac = trace * slope_mean - quad * inv_norm * (harmonic * harmonic * slope_inv + slope_mean)
    shared = 2.0 * inv_norm * quad
    d_x = weight * (along_x + cxx * grad_x - grad_x * shared)
    d_y = weight * (along_y + cyy * grad_y + cxy * grad_x - grad_y * shared)
    stack = jnp.concatenate([d_frac, d_x, d_y, jnp.zeros((SUB, 256), F32)], axis=0) * 0.5
    high, low = parts_of(stack, 2)
    place = place_lanes()
    flat, tilt = ([], [])
    for mask in masks:
        chosen = jnp.where(mask, 1.0, 0.0).astype(BF)
        both = dot(high * chosen, spread[...]) + dot(low * chosen, spread[...])
        flat.append(both[:72] + place * both[72:144])
        tilt.append(both[144:216])
    for q in range(SUB // 2):
        up, down = (None, None)
        for s in range(SLOPES):
            lean = (3.5 - q) * tilt[s]
            one, two = (slopes[s, q] * (flat[s] - lean), slopes[s, SUB - 1 - q] * (flat[s] + lean))
            up, down = (one, two) if up is None else (up + one, down + two)
        natural[pl.ds(q, CELLS, stride=SUB), :] = up
        natural[pl.ds(SUB - 1 - q, CELLS, stride=SUB), :] = down
    out[...] = natural[:WIDTH, :]
    pieces = []
    for block in range(3):
        count = 192 if block < 2 else 128
        if block == 0:
            window = jnp.concatenate([natural[WIDTH + RADIUS : WIDE, :], natural[:224, :]], axis=0)
        else:
            window = natural[192 * block - RADIUS : 192 * block + count + RADIUS, :]
        wide = dot(plain[:count, : count + 64], jnp.concatenate(parts_of(window, 2), axis=1))
        pieces.append((wide[:, :128] + wide[:, 128:]) * SCALE)
    result = jnp.concatenate(pieces, axis=0).T
    turned[...] = result
    to_near[...], to_far[...] = sides("xy", result[:RADIUS], result[HEIGHT - RADIUS :])


def emit_odd(grad, turned, out, result, partial, *scratch):
    @pl.when(odd("xy"))
    def _():
        emit(grad, turned, out, result, partial, *scratch)


def emit_even(grad, turned, out_before, result_before, out, result, partial, *scratch):
    @pl.when(jnp.logical_not(odd("xy")))
    def _():
        emit(grad, turned, out, result, partial, *scratch)


def emit(grad, turned, out, result, partial, whole, middle, sems):
    whole[...] = grad[...].T
    copies = [pltpu.make_async_copy(whole, out, sems.at[0])]
    copies[0].start()
    matrix = band(HEIGHT, HEIGHT + 2 * RADIUS)[:, RADIUS : RADIUS + HEIGHT]
    high, low = parts_of(turned[...], 2)
    total = (dot(matrix, high) + dot(matrix, low)) * SCALE
    middle[...] = total[RADIUS : HEIGHT - RADIUS]
    copies.append(pltpu.make_async_copy(middle, result.at[pl.ds(RADIUS, HEIGHT - 2 * RADIUS)], sems.at[1]))
    copies[1].start()
    partial[:RADIUS] = total[:RADIUS]
    partial[RADIUS:] = total[HEIGHT - RADIUS :]
    for copy in copies:
        copy.wait()


def last_body(near, far, partial_odd, partial_even, start, result, ends, sems):
    partial = jnp.where(odd("xy"), partial_odd[...], partial_even[...])
    before, after = sides("xy", near[...], far[...])
    matrix = band(RADIUS, 3 * RADIUS)
    copies = []
    for index, (rows, weights) in enumerate([(before, matrix[:, :RADIUS]), (after, matrix[:, 2 * RADIUS :])]):
        high, low = parts_of(rows, 2)
        ends[index] = partial[RADIUS * index : RADIUS * (index + 1)] + (dot(weights, high) + dot(weights, low)) * SCALE
        where = result.at[pl.ds((HEIGHT - RADIUS) * index, RADIUS)]
        copies.append(pltpu.make_async_copy(ends.at[index], where, sems.at[index]))
        copies[-1].start()
    for copy in copies:
        copy.wait()


def pairs(axis, start):
    return [(i, i + 1) for i in range(start, lax.axis_size(axis) - 1, 2)]


def back(steps):
    return [(j, i) for i, j in steps]


def swap(near, far, axis):
    inner, outer = (pairs(axis, 0), pairs(axis, 1))
    far = lax.ppermute(far, axis, outer + back(outer))
    return (lax.ppermute(near, axis, inner + back(inner)), far)


def steps(density, cotangent, slope, layer_block, block_eps):
    shapes = [(64, 128), (64, 128), (RADIUS, WIDTH), (RADIUS, WIDTH)]
    near, far, *rows = pl.pallas_call(
        columns_body,
        name="columns",
        out_shape=[jax.ShapeDtypeStruct(shape, F32) for shape in shapes],
        in_specs=[HBM],
        out_specs=[VMEM] * 4,
        scratch_shapes=[pltpu.VMEM((HEIGHT, 128), F32), pltpu.VMEM((HEIGHT, 128), F32), pltpu.SemaphoreType.DMA((4,))],
        compiler_params=pltpu.CompilerParams(vmem_limit_bytes=8 << 20),
        cost_estimate=pl.CostEstimate(flops=10**6, bytes_accessed=10**6, transcendentals=0),
    )(pltpu.with_memory_space_constraint(density, pltpu.HBM))
    near, far = swap(near, far, "gz")
    (send,) = pl.pallas_call(
        pack_body,
        name="pack",
        out_shape=[jax.ShapeDtypeStruct((4, ROWS, 128), F32)],
        in_specs=[HBM] * 4,
        out_specs=[HBM],
        scratch_shapes=[
            pltpu.SMEM((4,), jnp.int32),
            pltpu.SMEM((4,), jnp.int32),
            pltpu.SMEM((2, 4), F32),
            pltpu.VMEM((384, 256), F32),
            pltpu.VMEM((4, ROWS, 128), F32),
            pltpu.SemaphoreType.DMA((9,)),
        ],
        compiler_params=pltpu.CompilerParams(vmem_limit_bytes=60 * 1024 * 1024),
        cost_estimate=pl.CostEstimate(flops=10**6, bytes_accessed=10**6, transcendentals=0),
    )(slope, layer_block, block_eps.T, cotangent.reshape(384, 256))
    got = lax.all_to_all(send, "gz", 0, 0, tiled=True)
    edges = [(HEIGHT, 128), (RADIUS, WIDTH + 128), (RADIUS, WIDTH + 128)]
    halo, near, far = call(edges_body, edges, [], 10**5, 10**6, near, far, *rows)
    inner, outer = (pairs("xy", 0), pairs("xy", 1))
    down = lax.ppermute(far, "xy", outer)
    up = lax.ppermute(far, "xy", back(outer))
    near = lax.ppermute(near, "xy", inner + back(inner))
    shapes = [(WIDTH, HEIGHT), (HEIGHT, WIDTH), (RADIUS, WIDTH), (RADIUS, WIDTH)]
    scratch = [(SLOPES, SUB, CELLS, HEIGHT), (1088, 256), (WIDE, HEIGHT)]
    sizes = [(384, 192), (HEIGHT, 192), (192, 256), (256, 256), (256, HEIGHT)]
    constants = [jax.ShapeDtypeStruct(size, BF) for size in sizes]
    start = call(prior_body, [(WIDE, HEIGHT), *constants], [], 10**8, 10**6, density, halo)
    operands = (near, down, up, got, *start)
    grad, turned, near, far = call(adjoint_body, shapes, scratch, 2 * 10**8, 3 * 10**6, *operands)
    near, far = swap(near, far, "xy")
    whole = jax.ShapeDtypeStruct((HEIGHT, WIDTH), F32)

    def own_part(body, *before):
        return pl.pallas_call(
            body,
            out_shape=[whole, whole, jax.ShapeDtypeStruct((2 * RADIUS, WIDTH), F32)],
            in_specs=[VMEM] * 2 + [HBM] * len(before),
            out_specs=[HBM, HBM, VMEM],
            scratch_shapes=[
                pltpu.VMEM((HEIGHT, WIDTH), F32),
                pltpu.VMEM((HEIGHT - 2 * RADIUS, WIDTH), F32),
                pltpu.SemaphoreType.DMA((2,)),
            ],
            input_output_aliases={2 + index: index for index in range(len(before))},
            compiler_params=pltpu.CompilerParams(vmem_limit_bytes=LIMIT),
            cost_estimate=pl.CostEstimate(flops=10**8, bytes_accessed=10**6, transcendentals=0),
        )(grad, turned, *before)

    own, result, partial_odd = own_part(emit_odd)
    own, result, partial_even = own_part(emit_even, own, result)
    result = pl.pallas_call(
        last_body,
        name="last",
        out_shape=whole,
        in_specs=[VMEM] * 4 + [HBM],
        out_specs=HBM,
        scratch_shapes=[pltpu.VMEM((2, RADIUS, WIDTH), F32), pltpu.SemaphoreType.DMA((2,))],
        input_output_aliases={4: 0},
        compiler_params=pltpu.CompilerParams(vmem_limit_bytes=LIMIT),
        cost_estimate=pl.CostEstimate(flops=10**7, bytes_accessed=10**6, transcendentals=0),
    )(near, far, partial_odd, partial_even, result)
    return (own, result)


def solution(mesh):
    return jax.shard_map(
        steps,
        mesh=mesh,
        in_specs=(P("xy", "gz"), P(None, "gz", "xy", None), P("gz"), P("gz"), P()),
        out_specs=(P("xy", "gz"), P("xy", "gz")),
        check_vma=False,
    )
```

```python
import math

import jax
import jax.numpy as jnp
from jax import lax
from jax.experimental import pallas as pl
from jax.experimental.pallas import tpu as pltpu
from jax.sharding import PartitionSpec as P

SUB = 8
RADIUS = 32
SLOPES = 5
SCALE = 1.0 / float((RADIUS + 1) ** 2)
BF = jnp.bfloat16
F32 = jnp.float32
VMEM = pl.BlockSpec(memory_space=pltpu.VMEM)
SMEM = pl.BlockSpec(memory_space=pltpu.SMEM)
HBM = pl.BlockSpec(memory_space=pltpu.HBM)
LIMIT = 24 << 20

HEIGHT = 128
WIDTH = 512
WIDE = WIDTH + 2 * RADIUS
CELLS = WIDE // SUB
ROWS = 224


def iota(shape, dim):
    return lax.broadcasted_iota(jnp.int32, shape, dim)


def parts_of(value, count):
    parts = []
    for index in range(count):
        part = value.astype(BF)
        parts.append(part)
        if index + 1 < count:
            value = value - part.astype(F32)
    return parts


def band(rows, cols):
    offset = iota((rows, cols), 1) - iota((rows, cols), 0) - RADIUS
    return jnp.maximum(RADIUS + 1 - jnp.abs(offset), 0).astype(F32).astype(BF)


def dot(a, b):
    return jnp.dot(a, b, preferred_element_type=F32)


def place_lanes():
    return (iota((1, HEIGHT), 1) % SUB).astype(F32) - 3.5


def call(body, outs, scratch, flops, moved, *args, smem=()):
    return pl.pallas_call(
        body,
        out_shape=[out if hasattr(out, "dtype") else jax.ShapeDtypeStruct(out, F32) for out in outs],
        in_specs=[SMEM if index in smem else VMEM for index in range(len(args))],
        out_specs=[VMEM for _ in outs],
        scratch_shapes=[pltpu.VMEM(shape, F32) for shape in scratch],
        compiler_params=pltpu.CompilerParams(vmem_limit_bytes=LIMIT),
        cost_estimate=pl.CostEstimate(flops=flops, bytes_accessed=moved, transcendentals=0),
    )(*args)


def pack_body(slope_hbm, block_hbm, eps_hbm, cot_hbm, send_hbm, slope, block, eps, cot, send, sems):
    small = [
        pltpu.make_async_copy(source, target, sems.at[3 + index])
        for index, (source, target) in enumerate([(slope_hbm, slope), (block_hbm, block), (eps_hbm, eps)])
    ]
    slabs = [
        pltpu.make_async_copy(cot_hbm.at[pl.ds(128 * slab, 128)], cot.at[pl.ds(128 * slab, 128)], sems.at[slab])
        for slab in range(3)
    ]
    for copy in slabs + small:
        copy.start()
    low = iota((SUB, HEIGHT), 0) < 4
    zero = jnp.zeros((SUB, HEIGHT), F32)
    outs = []

    def put(first, rows):
        copy = pltpu.make_async_copy(
            send.at[:, pl.ds(first, rows)], send_hbm.at[:, pl.ds(first, rows)], sems.at[6 + len(outs)]
        )
        copy.start()
        outs.append(copy)

    for slab in range(3):
        slabs[slab].wait()
        turned = cot[slab * 128 : slab * 128 + 128, :].T
        for owner in range(4):
            first, base = (64 * owner, 72 * slab)
            send[owner, base : base + 64, :] = turned[first : first + 64]
            after = zero if owner == 3 else turned[first + 64 : first + 72]
            before = zero if owner == 0 else turned[first - 8 : first]
            send[owner, base + 64 : base + 72, :] = jnp.where(low, after, before)
        if slab < 2:
            put(72 * slab, 72)
    for copy in small:
        copy.wait()
    layer = (iota((SUB, HEIGHT), 1) % 64) // 16
    row = iota((SUB, HEIGHT), 0)
    table = zero
    for index in range(4):
        one = eps[0, block[index]]
        two = eps[1, block[index]]
        level = slope[index].astype(F32)
        column = jnp.where(row == 0, level, jnp.where(row == 1, one, jnp.where(row == 2, two, 0.0)))
        table = jnp.where(layer == index, column, table)
    for owner in range(4):
        send[owner, 216:224, :] = table
    put(144, 80)
    for copy in outs:
        copy.wait()


def odd(axis):
    return lax.rem(lax.axis_index(axis), 2) == 1


def sides(axis, near, far):
    return (jnp.where(odd(axis), near, far), jnp.where(odd(axis), far, near))


def low_lanes():
    return iota((1, 128), 1) < 64


def columns_body(own, to_near, to_far, rows_near, rows_far):
    begin, end = (own[:, :128], own[:, WIDTH - 128 :])
    first = jnp.where(low_lanes(), begin[:64], pltpu.roll(begin[64:], 64, 1))
    last = jnp.where(low_lanes(), pltpu.roll(end[:64], 64, 1), end[64:])
    to_near[...], to_far[...] = sides("gz", first, last)
    rows_near[...], rows_far[...] = sides("xy", own[:RADIUS], own[HEIGHT - RADIUS :])


def edges_body(near, far, rows_near, rows_far, halo, to_near, to_far):
    before, after = sides("gz", near[...], far[...])
    halo[:64] = jnp.where(low_lanes(), after, pltpu.roll(before, 64, 1))
    halo[64:] = jnp.where(low_lanes(), pltpu.roll(after, 64, 1), before)
    first, last = (slice(0, RADIUS), slice(HEIGHT - RADIUS, HEIGHT))
    to_near[:, :WIDTH] = rows_near[...]
    to_far[:, :WIDTH] = rows_far[...]
    to_near[:, WIDTH:], to_far[:, WIDTH:] = sides("xy", halo[first, :], halo[last, :])


def prior_body(own, halo, start, across, ahead, plain, pool, spread):
    middle = jnp.concatenate([own[...], halo[...]], axis=1)
    matrix = band(HEIGHT, HEIGHT + 2 * RADIUS)[:, RADIUS : RADIUS + HEIGHT]
    total = None
    for part in parts_of(middle, 3):
        term = dot(matrix, part)
        total = term if total is None else total + term
    turned = total.T
    padded = jnp.concatenate([turned[WIDTH + 64 :], turned[: WIDTH + 64]], axis=0)
    padded = jnp.concatenate(parts_of(padded, 3), axis=1)
    matrix = band(192, 256)
    plain[...] = matrix
    for block in range(3):
        wide = dot(matrix, padded[192 * block : 192 * block + 256])
        keep(start, block, wide[:, :128] + wide[:, 128:256] + wide[:, 256:])
    offset = iota((384, 192), 0) - iota((384, 192), 1) - 3 * RADIUS
    across[...] = jnp.maximum(RADIUS + 1 - jnp.abs(offset), 0).astype(F32).astype(BF)
    row = iota((HEIGHT, 192), 1) % 64
    offset = row + jnp.where(row < RADIUS, -RADIUS, 3 * RADIUS) - iota((HEIGHT, 192), 0)
    ahead[...] = jnp.maximum(RADIUS + 1 - jnp.abs(offset), 0).astype(F32).astype(BF)
    base = (iota((128, 256), 0) // SUB == iota((128, 256), 1) % 16).astype(F32).astype(BF)
    pool[...] = jnp.concatenate([base, base], axis=0)
    spread[...] = (iota((256, HEIGHT), 0) % 16 == iota((256, HEIGHT), 1) // SUB).astype(F32).astype(BF)


def places(block):
    first = 192 * block - RADIUS
    return [(0, RADIUS, WIDTH + RADIUS), (RADIUS, 192, 0)] if block == 0 else [(0, 192, first)]


def keep(target, block, value):
    for begin, end, first in places(block):
        target[first : first + end - begin, :] = value[begin:end]


def forward(near, down, up, start, across, ahead, pool, slopes, pooled, natural):
    before, after = sides("xy", near[...], jnp.where(odd("xy"), up[...], down[...]))
    rows = jnp.concatenate(parts_of(jnp.concatenate([before, after], axis=0), 3), axis=0)
    windows = [jnp.concatenate([rows[:, WIDTH:], rows[:, :256]], axis=1), rows[:, 128:384], rows[:, 256:]]
    for block, window in enumerate(windows):
        weights = across[64:320, :] if block == 1 else across[...]
        wide = dot(window, weights)
        beside = parts_of(wide[:64] + wide[64:128] + wide[128:], 3)
        added = dot(ahead[...], jnp.concatenate(beside, axis=0)).T
        own = jnp.concatenate([start[first : first + end - begin, :] for begin, end, first in places(block)], axis=0)
        keep(natural, block, jnp.exp(16.0 - (32.0 * SCALE * SCALE) * (own + added)))
    expo = [natural[pl.ds(q, CELLS, stride=SUB), :] for q in range(SUB)]
    place = place_lanes()
    stacks = []
    for s in range(SLOPES):
        factor = math.exp(0.64 * (s - 2))
        mean, slant = (None, None)
        for q in range(SUB // 2):
            pair = []
            for row in (q, SUB - 1 - q):
                scaled = factor * expo[row]
                fill = 1.0 / (1.0 + scaled)
                slopes[s, row] = fill * fill * scaled
                pair.append(fill)
            both, apart = (pair[0] + pair[1], (3.5 - q) * (pair[1] - pair[0]))
            mean = both if mean is None else mean + both
            slant = apart if slant is None else slant + apart
        stacks += [mean, mean * place, slant]
    stacks.append(jnp.zeros((SUB, HEIGHT), F32))
    rows = jnp.concatenate(parts_of(jnp.concatenate(stacks, axis=0), 2), axis=1)
    pooled[...] = dot(rows, pool[...])


def adjoint_body(near, down, up, got, start, across, ahead, plain, pool, spread, out, turned, to_near, to_far, slopes, pooled, natural):
    forward(near, down, up, start, across, ahead, pool, slopes, pooled, natural)
    half = low_lanes()

    def pair(a, b):
        return jnp.where(half, a, b)

    def line(row):
        value = [got[g, row : row + 1, :] for g in range(4)]
        return jnp.concatenate([pair(value[0], value[1]), pair(value[2], value[3])], axis=1)

    level, eps_one, eps_two = (line(216), line(217), line(218))
    comps = []
    for slab in range(3):
        value = [got[g, 72 * slab : 72 * slab + 72, :] for g in range(4)]
        swapped = [pltpu.roll(v, 64, 1) for v in value]
        comps.append(jnp.concatenate([pair(value[0], swapped[1]), pair(value[2], swapped[3])], axis=1))
        comps.append(jnp.concatenate([pair(swapped[0], value[1]), pair(swapped[2], value[3])], axis=1))
    cxx, cyy, czz, cxy, cxz, cyz = comps
    frac = jnp.zeros((CELLS, 256), F32)
    grad_x = jnp.zeros((CELLS, 256), F32)
    grad_y = jnp.zeros((CELLS, 256), F32)
    masks = []
    for s in range(SLOPES):
        mask = level == float(s)
        masks.append(mask)
        frac = jnp.where(mask, pooled[216 * s : 216 * s + 72, :], frac)
        grad_x = jnp.where(mask, pooled[216 * s + 72 : 216 * s + 144, :], grad_x)
        grad_y = jnp.where(mask, pooled[216 * s + 144 : 216 * s + 216, :], grad_y)
    frac, grad_x, grad_y = (value * (1.0 / 64.0) for value in (frac, grad_x, grad_y))
    lift = 0.2 * (1.0 + level)
    slope_mean = eps_one - eps_two
    inv_two = 1.0 / eps_two
    slope_inv = 1.0 / eps_one - inv_two
    mean_eps = eps_two + frac * slope_mean
    harmonic = 1.0 / (inv_two + frac * slope_inv)
    inv_norm = 1.0 / (grad_x * grad_x + grad_y * grad_y + lift * lift)
    weight = (harmonic - mean_eps) * inv_norm
    along_x = cxx * grad_x + cxy * grad_y + cxz * lift
    along_y = cyy * grad_y + cyz * lift
    quad = grad_x * along_x + grad_y * along_y + czz * (lift * lift)
    trace = cxx + cyy + czz
    d_frac = trace * slope_mean - quad * inv_norm * (harmonic * harmonic * slope_inv + slope_mean)
    shared = 2.0 * inv_norm * quad
    d_x = weight * (along_x + cxx * grad_x - grad_x * shared)
    d_y = weight * (along_y + cyy * grad_y + cxy * grad_x - grad_y * shared)
    stack = jnp.concatenate([d_frac, d_x, d_y, jnp.zeros((SUB, 256), F32)], axis=0) * 0.5
    high, low = parts_of(stack, 2)
    place = place_lanes()
    flat, tilt = ([], [])
    for mask in masks:
        chosen = jnp.where(mask, 1.0, 0.0).astype(BF)
        both = dot(high * chosen, spread[...]) + dot(low * chosen, spread[...])
        flat.append(both[:72] + place * both[72:144])
        tilt.append(both[144:216])
    for q in range(SUB // 2):
        up, down = (None, None)
        for s in range(SLOPES):
            lean = (3.5 - q) * tilt[s]
            one, two = (slopes[s, q] * (flat[s] - lean), slopes[s, SUB - 1 - q] * (flat[s] + lean))
            up, down = (one, two) if up is None else (up + one, down + two)
        natural[pl.ds(q, CELLS, stride=SUB), :] = up
        natural[pl.ds(SUB - 1 - q, CELLS, stride=SUB), :] = down
    out[...] = natural[:WIDTH, :]
    pieces = []
    for block in range(3):
        count = 192 if block < 2 else 128
        if block == 0:
            window = jnp.concatenate([natural[WIDTH + RADIUS : WIDE, :], natural[:224, :]], axis=0)
        else:
            window = natural[192 * block - RADIUS : 192 * block + count + RADIUS, :]
        wide = dot(plain[:count, : count + 64], jnp.concatenate(parts_of(window, 2), axis=1))
        pieces.append((wide[:, :128] + wide[:, 128:]) * SCALE)
    result = jnp.concatenate(pieces, axis=0).T
    turned[...] = result
    to_near[...], to_far[...] = sides("xy", result[:RADIUS], result[HEIGHT - RADIUS :])


def emit_odd(grad, turned, out, result, partial, *scratch):
    @pl.when(odd("xy"))
    def _():
        emit(grad, turned, out, result, partial, *scratch)


def emit_even(grad, turned, out_before, result_before, out, result, partial, *scratch):
    @pl.when(jnp.logical_not(odd("xy")))
    def _():
        emit(grad, turned, out, result, partial, *scratch)


def emit(grad, turned, out, result, partial, whole, middle, sems):
    whole[...] = grad[...].T
    copies = [pltpu.make_async_copy(whole, out, sems.at[0])]
    copies[0].start()
    matrix = band(HEIGHT, HEIGHT + 2 * RADIUS)[:, RADIUS : RADIUS + HEIGHT]
    high, low = parts_of(turned[...], 2)
    total = (dot(matrix, high) + dot(matrix, low)) * SCALE
    middle[...] = total[RADIUS : HEIGHT - RADIUS]
    copies.append(pltpu.make_async_copy(middle, result.at[pl.ds(RADIUS, HEIGHT - 2 * RADIUS)], sems.at[1]))
    copies[1].start()
    partial[:RADIUS] = total[:RADIUS]
    partial[RADIUS:] = total[HEIGHT - RADIUS :]
    for copy in copies:
        copy.wait()


def last_body(near, far, partial_odd, partial_even, start, result, ends, sems):
    partial = jnp.where(odd("xy"), partial_odd[...], partial_even[...])
    before, after = sides("xy", near[...], far[...])
    matrix = band(RADIUS, 3 * RADIUS)
    copies = []
    for index, (rows, weights) in enumerate([(before, matrix[:, :RADIUS]), (after, matrix[:, 2 * RADIUS :])]):
        high, low = parts_of(rows, 2)
        ends[index] = partial[RADIUS * index : RADIUS * (index + 1)] + (dot(weights, high) + dot(weights, low)) * SCALE
        where = result.at[pl.ds((HEIGHT - RADIUS) * index, RADIUS)]
        copies.append(pltpu.make_async_copy(ends.at[index], where, sems.at[index]))
        copies[-1].start()
    for copy in copies:
        copy.wait()


def pairs(axis, start):
    return [(i, i + 1) for i in range(start, lax.axis_size(axis) - 1, 2)]


def back(steps):
    return [(j, i) for i, j in steps]


def swap(near, far, axis):
    inner, outer = (pairs(axis, 0), pairs(axis, 1))
    far = lax.ppermute(far, axis, outer + back(outer))
    return (lax.ppermute(near, axis, inner + back(inner)), far)


def steps(density, cotangent, slope, layer_block, block_eps):
    shapes = [(64, 128), (64, 128), (RADIUS, WIDTH), (RADIUS, WIDTH)]
    near, far, *rows = call(columns_body, shapes, [], 10**5, 10**6, density)
    near, far = swap(near, far, "gz")
    (send,) = pl.pallas_call(
        pack_body,
        name="pack",
        out_shape=[jax.ShapeDtypeStruct((4, ROWS, 128), F32)],
        in_specs=[HBM] * 4,
        out_specs=[HBM],
        scratch_shapes=[
            pltpu.SMEM((4,), jnp.int32),
            pltpu.SMEM((4,), jnp.int32),
            pltpu.SMEM((2, 4), F32),
            pltpu.VMEM((384, 256), F32),
            pltpu.VMEM((4, ROWS, 128), F32),
            pltpu.SemaphoreType.DMA((9,)),
        ],
        compiler_params=pltpu.CompilerParams(vmem_limit_bytes=60 * 1024 * 1024),
        cost_estimate=pl.CostEstimate(flops=10**6, bytes_accessed=10**6, transcendentals=0),
    )(slope, layer_block, block_eps.T, cotangent.reshape(384, 256))
    got = lax.all_to_all(send, "gz", 0, 0, tiled=True)
    edges = [(HEIGHT, 128), (RADIUS, WIDTH + 128), (RADIUS, WIDTH + 128)]
    halo, near, far = call(edges_body, edges, [], 10**5, 10**6, near, far, *rows)
    inner, outer = (pairs("xy", 0), pairs("xy", 1))
    down = lax.ppermute(far, "xy", outer)
    up = lax.ppermute(far, "xy", back(outer))
    near = lax.ppermute(near, "xy", inner + back(inner))
    shapes = [(WIDTH, HEIGHT), (HEIGHT, WIDTH), (RADIUS, WIDTH), (RADIUS, WIDTH)]
    scratch = [(SLOPES, SUB, CELLS, HEIGHT), (1088, 256), (WIDE + SUB, HEIGHT)]
    sizes = [(384, 192), (HEIGHT, 192), (192, 256), (256, 256), (256, HEIGHT)]
    constants = [jax.ShapeDtypeStruct(size, BF) for size in sizes]
    start = call(prior_body, [(WIDE, HEIGHT), *constants], [], 10**8, 10**6, density, halo)
    operands = (near, down, up, got, *start)
    grad, turned, near, far = call(adjoint_body, shapes, scratch, 2 * 10**8, 3 * 10**6, *operands)
    near, far = swap(near, far, "xy")
    whole = jax.ShapeDtypeStruct((HEIGHT, WIDTH), F32)

    def own_part(body, *before):
        return pl.pallas_call(
            body,
            out_shape=[whole, whole, jax.ShapeDtypeStruct((2 * RADIUS, WIDTH), F32)],
            in_specs=[VMEM] * 2 + [HBM] * len(before),
            out_specs=[HBM, HBM, VMEM],
            scratch_shapes=[
                pltpu.VMEM((HEIGHT, WIDTH), F32),
                pltpu.VMEM((HEIGHT - 2 * RADIUS, WIDTH), F32),
                pltpu.SemaphoreType.DMA((2,)),
            ],
            input_output_aliases={2 + index: index for index in range(len(before))},
            compiler_params=pltpu.CompilerParams(vmem_limit_bytes=LIMIT),
            cost_estimate=pl.CostEstimate(flops=10**8, bytes_accessed=10**6, transcendentals=0),
        )(grad, turned, *before)

    own, result, partial_odd = own_part(emit_odd)
    own, result, partial_even = own_part(emit_even, own, result)
    result = pl.pallas_call(
        last_body,
        name="last",
        out_shape=whole,
        in_specs=[VMEM] * 4 + [HBM],
        out_specs=HBM,
        scratch_shapes=[pltpu.VMEM((2, RADIUS, WIDTH), F32), pltpu.SemaphoreType.DMA((2,))],
        input_output_aliases={4: 0},
        compiler_params=pltpu.CompilerParams(vmem_limit_bytes=LIMIT),
        cost_estimate=pl.CostEstimate(flops=10**7, bytes_accessed=10**6, transcendentals=0),
    )(near, far, partial_odd, partial_even, result)
    return (own, result)


def solution(mesh):
    return jax.shard_map(
        steps,
        mesh=mesh,
        in_specs=(P("xy", "gz"), P(None, "gz", "xy", None), P("gz"), P("gz"), P()),
        out_specs=(P("xy", "gz"), P("xy", "gz")),
        check_vma=False,
    )
```
